32 devices in a mesh: px: 8 (over y, x, core), py: 4 (over z).
Axes of the slice: x: 2, y: 2, z: 4, core: 2. Of those that a mesh axis runs over, the one named last changes fastest.
Arguments:
- velocity: float32 [8, 1024, 1024], P(None, 'px', 'py'), may hold values from -6 to 6
- forcing: bfloat16 [8, 1024, 1024], P(None, 'px', 'py'), may hold values from -6 to 6
- cross_x: bfloat16 [8, 1024, 1024], P(None, 'px', 'py'), may hold values from -1.5 to 1.5
- cross_y: bfloat16 [8, 1024, 1024], P(None, 'px', 'py'), may hold values from -1.5 to 1.5
- inv_x: bfloat16 [8, 1024, 1024], P('px'), may hold values from -1 to 2, as said below
- inv_y: bfloat16 [8, 1024, 1024], P('px'), may hold values from -1 to 2, as said below
Outputs:
- velocity_new: float32 [8, 1024, 1024], P(None, 'px', 'py')
The draws below stay inside these ranges and needn't reach their ends.
Inputs may be any that keep to these rules, and one draw needn't show every extreme that they name: `inv_x`: a dense matrix for each level. `inv_y`: a dense matrix for each level.
All inputs are finite; a program needn't handle non-finite values.
Results may differ from the reference program's by a relative error of at most 0.0052.
Values may be sent and summed in bfloat16 or wider, within the bound.
A program may use at most 64 MiB of HBM per device.

```python
import math
import jax
import jax.numpy as jnp
from jax import lax

NX = 1024
NY = 1024
NZ = 8


def dominant_matrix(key, levels, order):
    key_diag, key_noise = jax.random.split(key)
    diagonal = jax.random.uniform(key_diag, (levels, order), jnp.float32, 0.8, 1.2)
    noise = jax.random.normal(key_noise, (levels, order, order), jnp.float32) * (0.6 / math.sqrt(order))
    identity = jnp.eye(order, dtype=jnp.float32)
    whole = noise * (1.0 - identity) + identity * diagonal[:, :, None]
    return whole.astype(jnp.bfloat16)


def draw_inv_x(key, part):
    return dominant_matrix(jax.random.fold_in(key, 11), NZ, NX)


def draw_inv_y(key, part):
    return dominant_matrix(jax.random.fold_in(key, 23), NZ, NY)


def block_scale(key, shape, shards, low, largest):
    def one(axis_at, parts):
        heights = jax.random.uniform(jax.random.fold_in(jax.random.fold_in(key, 6), axis_at), (parts,), jnp.float32, low / len(shards), largest / len(shards))
        return jnp.repeat(jnp.exp(heights), shape[axis_at] // parts).reshape((-1,) + (1,) * (len(shape) - axis_at - 1))

    factor_of = one(*shards[0])
    for cut in shards[1:]:
        factor_of = factor_of * one(*cut)
    return factor_of


def scatter_about(own_key, dims, scale, reach, cuts=(), kind=jnp.bfloat16):
    values = scale * jax.random.normal(own_key, dims, jnp.float32)
    if cuts:
        values = values * block_scale(own_key, dims, cuts, -0.22, 0.18)
    return jnp.clip(values, -reach, reach).astype(kind)


def setup_inputs(seed: int = 0) -> dict:
    streams_of = jax.random.split(jax.random.key(seed), 7)
    velocity = scatter_about(streams_of[0], (NZ, NX, NY), 1.0, 6.0, ((1, 8), (2, 4)), jnp.float32)
    forcing = scatter_about(streams_of[1], (NZ, NX, NY), 1.0, 6.0, ((1, 8), (2, 4)))
    cross_x = jnp.clip(jax.random.uniform(streams_of[2], (NZ, NX, NY), jnp.float32, -1.5, 1.5) * block_scale(streams_of[2], (NZ, NX, NY), ((1, 8), (2, 4)), -0.4, 0.0), -1.5, 1.5).astype(jnp.bfloat16)
    cross_y = jnp.clip(jax.random.uniform(streams_of[3], (NZ, NX, NY), jnp.float32, -1.5, 1.5) * block_scale(streams_of[3], (NZ, NX, NY), ((1, 8), (2, 4)), -0.4, 0.0), -1.5, 1.5).astype(jnp.bfloat16)
    inv_x = draw_inv_x(jax.random.fold_in(streams_of[6], 71), 0)
    inv_y = draw_inv_y(jax.random.fold_in(streams_of[6], 71), 0)
    return {"velocity": velocity, "forcing": forcing, "cross_x": cross_x, "cross_y": cross_y, "inv_x": inv_x, "inv_y": inv_y}


time_step = 0.25


def reference(velocity, forcing, cross_x, cross_y, inv_x, inv_y):
    x_plus = jnp.roll(velocity, -1, 1)
    x_minus = jnp.roll(velocity, 1, 1)
    y_plus = jnp.roll(velocity, -1, 2)
    y_minus = jnp.roll(velocity, 1, 2)
    z_padded = jnp.pad(velocity, ((1, 1), (0, 0), (0, 0)))
    laplace = x_plus + x_minus + y_plus + y_minus - 4.0 * velocity + z_padded[2:] + z_padded[:-2] - 2.0 * velocity
    slope_x = jnp.pad(0.5 * (x_plus - x_minus), ((1, 1), (0, 0), (0, 0)))
    slope_y = jnp.pad(0.5 * (y_plus - y_minus), ((1, 1), (0, 0), (0, 0)))
    mixed_x = 0.5 * (slope_x[2:] - slope_x[:-2])
    mixed_y = 0.5 * (slope_y[2:] - slope_y[:-2])
    total = laplace + cross_x.astype(jnp.float32) * mixed_x + cross_y.astype(jnp.float32) * mixed_y + forcing.astype(jnp.float32)
    rhs = (time_step * total).astype(jnp.bfloat16)

    def sweep_x(pair):
        inverse, level_rhs = pair
        return jnp.dot(inverse, level_rhs, preferred_element_type=jnp.float32).astype(jnp.bfloat16)

    section_one = lax.map(sweep_x, (inv_x, rhs))

    def sweep_y(pair):
        inverse, level_rhs = pair
        return jnp.dot(level_rhs, inverse.T, preferred_element_type=jnp.float32)

    section_two = lax.map(sweep_y, (inv_y, section_one))
    return velocity + section_two
```

```python
import functools

import jax
import jax.numpy as jnp
from jax import lax
from jax.experimental import pallas as pl
from jax.experimental.pallas import tpu as pltpu
from jax.sharding import PartitionSpec as P

time_step = 0.25


def with_halo(cells, sides, width):
    for axis, dim in sides:
        count = lax.axis_size(axis)
        head = lax.slice_in_dim(cells, 0, width, axis=dim)
        tail = lax.slice_in_dim(cells, cells.shape[dim] - width, cells.shape[dim], axis=dim)
        cells = jnp.concatenate(
            [
                lax.ppermute(tail, axis, [(i, (i + 1) % count) for i in range(count)]),
                cells,
                lax.ppermute(head, axis, [((i + 1) % count, i) for i in range(count)]),
            ],
            axis=dim,
        )
    return cells


def shards(velocity, forcing, cross_x, cross_y, inv_x, inv_y):
    padded = with_halo(velocity, (("px", 1), ("py", 2)), 1)
    x_plus = padded[:, 2:, 1:-1]
    x_minus = padded[:, :-2, 1:-1]
    y_plus = padded[:, 1:-1, 2:]
    y_minus = padded[:, 1:-1, :-2]
    z_padded = jnp.pad(velocity, ((1, 1), (0, 0), (0, 0)))
    laplace = (
        x_plus
        + x_minus
        + y_plus
        + y_minus
        - 4.0 * velocity
        + z_padded[2:]
        + z_padded[:-2]
        - 2.0 * velocity
    )
    slope_x = jnp.pad(0.5 * (x_plus - x_minus), ((1, 1), (0, 0), (0, 0)))
    slope_y = jnp.pad(0.5 * (y_plus - y_minus), ((1, 1), (0, 0), (0, 0)))
    mixed_x = 0.5 * (slope_x[2:] - slope_x[:-2])
    mixed_y = 0.5 * (slope_y[2:] - slope_y[:-2])
    total = (
        laplace
        + cross_x.astype(jnp.float32) * mixed_x
        + cross_y.astype(jnp.float32) * mixed_y
        + forcing.astype(jnp.float32)
    )
    rhs = (time_step * total).astype(jnp.bfloat16)
    section_one = jnp.einsum(
        "lab,lbk->lak",
        inv_x,
        lax.all_to_all(rhs, "px", split_axis=0, concat_axis=1, tiled=True),
        preferred_element_type=jnp.float32,
    ).astype(jnp.bfloat16)
    y_lines = lax.all_to_all(section_one, "py", split_axis=1, concat_axis=2, tiled=True)
    section_two = jnp.einsum("lxb,lab->lxa", y_lines, inv_y, preferred_element_type=jnp.float32)
    settled = lax.all_to_all(
        lax.all_to_all(section_two, "py", split_axis=2, concat_axis=1, tiled=True),
        "px",
        split_axis=1,
        concat_axis=0,
        tiled=True,
    )
    return velocity + settled


def send(src, dst, send_sem, recv_sem, target):
    return pltpu.make_async_remote_copy(
        src_ref=src,
        dst_ref=dst,
        send_sem=send_sem,
        recv_sem=recv_sem,
        device_id=target,
        device_id_type=pl.DeviceIdType.MESH,
    )


def kernel(
    npx,
    npy,
    vel_hbm,
    frc_hbm,
    cx_hbm,
    cy_hbm,
    ix_hbm,
    iy_hbm,
    out,
    vel,
    frc,
    cx,
    cy,
    ix,
    iy,
    x_send,
    x_recv,
    x_mixed,
    y_send,
    y_recv,
    slope_x,
    slope_y,
    lap,
    rhs,
    lines,
    cross,
    mid,
    two,
    fin,
    fix_send,
    fix_recv,
    fix_rows,
    fix_cols,
    load_sem,
    halo_send,
    halo_recv,
    rhs_send,
    own_send,
    fix_sent,
    fix_own,
    fix_come,
    lines_come,
    cross_come,
    mid_send,
    two_send,
    two_own,
    fin_send,
    out_recv,
):
    me = lax.axis_index("px")
    my = lax.axis_index("py")
    levels, rows, cols = vel.shape
    part = rows // npy
    order_x, order_y = npx * rows, npy * cols
    x_first = lax.rem(me, 2) == 0
    pieces = [(vel_hbm, vel), (frc_hbm, frc), (cx_hbm, cx), (cy_hbm, cy), (ix_hbm, ix), (iy_hbm, iy)]
    loads = [pltpu.make_async_copy(a, b, load_sem.at[i]) for i, (a, b) in enumerate(pieces)]
    loads[0].start()

    barrier = pltpu.get_barrier_semaphore()

    def greet(at, _):
        other = lax.rem(me * npy + my + at, npx * npy)
        pl.semaphore_signal(
            barrier, inc=1, device_id={"px": other // npy, "py": lax.rem(other, npy)}, device_id_type=pl.DeviceIdType.MESH
        )
        return 0

    lax.fori_loop(1, npx * npy, greet, 0)
    fix_rows[...] = jnp.zeros_like(fix_rows)
    loads[0].wait()
    for load in loads[1:]:
        load.start()
    lane = lax.broadcasted_iota(jnp.int32, (rows, 128), 1)
    zero = jnp.zeros((rows, 128), jnp.float32)

    def ends_of(ref):
        def one_level(level, faces):
            first, last = faces
            first = jnp.where(lane == level, ref[level, :, 0:1].astype(jnp.float32), first)
            last = jnp.where(lane == level, ref[level, :, cols - 1 : cols].astype(jnp.float32), last)
            return first, last

        first, last = lax.fori_loop(0, levels, one_level, (zero, zero))
        return jnp.transpose(first)[:levels], jnp.transpose(last)[:levels]

    y_send[0], y_send[1] = ends_of(vel)
    for level in range(levels):
        x_send[0, level : level + 1, :] = vel[level, 0:1, :]
        x_send[1, level : level + 1, :] = vel[level, rows - 1 : rows, :]
    pl.semaphore_wait(barrier, npx * npy - 1)

    up_x, down_x = lax.rem(me + 1, npx), lax.rem(me + npx - 1, npx)
    up_y, down_y = lax.rem(my + 1, npy), lax.rem(my + npy - 1, npy)
    halos_y = [
        send(y_send.at[1], y_recv.at[0], halo_send.at[0], halo_recv.at[0], {"py": up_y}),
        send(y_send.at[0], y_recv.at[1], halo_send.at[1], halo_recv.at[1], {"py": down_y}),
    ]
    halos_x = [
        send(x_send.at[1], x_recv.at[0], halo_send.at[2], halo_recv.at[2], {"px": up_x}),
        send(x_send.at[0], x_recv.at[1], halo_send.at[3], halo_recv.at[3], {"px": down_x}),
    ]
    for halo in halos_y + halos_x:
        halo.start()
    row_at = lax.broadcasted_iota(jnp.int32, (rows, cols), 0)
    col_at = lax.broadcasted_iota(jnp.int32, (rows, cols), 1)
    blank = jnp.zeros((rows, cols), jnp.float32)
    for edge in (0, levels + 1):
        slope_x[edge] = blank
        slope_y[edge] = blank

    def slopes(level, _):
        now = vel[level]
        x_minus = jnp.where(row_at == 0, 0.0, pltpu.roll(now, 1, 0))
        x_plus = jnp.where(row_at == rows - 1, 0.0, pltpu.roll(now, rows - 1, 0))
        y_minus = jnp.where(col_at == 0, 0.0, pltpu.roll(now, 1, 1))
        y_plus = jnp.where(col_at == cols - 1, 0.0, pltpu.roll(now, cols - 1, 1))
        slope_x[level + 1] = 0.5 * (x_plus - x_minus)
        slope_y[level + 1] = 0.5 * (y_plus - y_minus)
        lap[level] = x_plus + x_minus + y_plus + y_minus - 4.0 * now
        return 0

    lax.fori_loop(0, levels, slopes, 0)
    for load in loads[1:4]:
        load.wait()

    def strip(at):
        return pl.ds(pl.multiple_of(at * cols, cols), cols)

    def rows_of(at):
        return pl.ds(pl.multiple_of(at * part, part), part)

    def inner(level):
        above = jnp.minimum(level + 1, levels - 1)
        below = jnp.maximum(level - 1, 0)
        z_plus = jnp.where(level < levels - 1, 1.0, 0.0) * vel[above]
        z_minus = jnp.where(level > 0, 1.0, 0.0) * vel[below]
        total = lap[level] + z_plus + z_minus - 2.0 * vel[level]
        total += cx[level].astype(jnp.float32) * (0.5 * (slope_x[level + 2] - slope_x[level]))
        total += cy[level].astype(jnp.float32) * (0.5 * (slope_y[level + 2] - slope_y[level]))
        total += frc[level].astype(jnp.float32)
        lap[level] = total
        rhs[level] = (time_step * total).astype(jnp.bfloat16)

    def to_cross(level, other):
        src, dst = rhs.at[level, rows_of(other), :], cross.at[me, :, strip(my)]

        def away(sem):
            return send(src, dst, sem, cross_come, {"px": level, "py": other})

        @pl.when(level != me)
        def _():
            away(rhs_send.at[level]).start()

        @pl.when((level == me) & (other != my))
        def _():
            away(own_send.at[other]).start()

        @pl.when((level == me) & (other == my))
        def _():
            pltpu.make_async_copy(src, dst, cross_come).start()

    def to_lines(level):
        @pl.when(level != me)
        def _():
            send(rhs.at[level], lines.at[me], rhs_send.at[level], lines_come, {"px": level}).start()

        @pl.when(level == me)
        def _():
            pltpu.make_async_copy(rhs.at[level], lines.at[me], lines_come).start()

    pairs = npx // 2

    def level_of(at, odd):
        return 2 * lax.rem(me // 2 + 1 + at, pairs) + odd

    def early(at, _):
        level = level_of(at, 1)
        inner(level)
        for other in range(1, npy - 1):
            to_cross(level, other)
        return 0

    def early_even(at, _):
        inner(level_of(at, 0))
        return 0

    lax.fori_loop(0, pairs, early, 0)
    lax.fori_loop(0, pairs, early_even, 0)
    for halo in halos_x:
        halo.wait_recv()

    def level_slope(face):
        at = lax.broadcasted_iota(jnp.int32, face.shape, 0)
        lower = jnp.where(at == 0, 0.0, pltpu.roll(face, 1, 0))
        upper = jnp.where(at == levels - 1, 0.0, pltpu.roll(face, levels - 1, 0))
        return 0.25 * (upper - lower)

    x_mixed[0] = -level_slope(x_recv[0])
    x_mixed[1] = level_slope(x_recv[1])
    slab_at = lax.broadcasted_iota(jnp.int32, (16, cols), 0)

    def fix_x(level):
        for end, first in enumerate((0, rows - 16)):
            slab = slice(first, first + 16)
            face = x_recv[end, pl.ds(level, 1), :] + cx[level, slab, :].astype(jnp.float32) * x_mixed[end, pl.ds(level, 1), :]
            total = lap[level, slab, :] + jnp.where(slab_at == 15 * end, face, 0.0)
            lap[level, slab, :] = total
            rhs[level, slab, :] = (time_step * total).astype(jnp.bfloat16)

    def late(at, _):
        level = level_of(at, 1)
        fix_x(level)
        for other in sorted({0, npy - 1}):
            to_cross(level, other)
        return 0

    def late_even(at, _):
        level = level_of(at, 0)
        fix_x(level)
        to_lines(level)
        return 0

    lax.fori_loop(0, pairs, late, 0)
    lax.fori_loop(0, pairs, late_even, 0)

    near, far = ends_of(lap), ends_of(cy)
    for halo in halos_y:
        halo.wait_recv()
    for end in range(2):
        face = y_recv[end]
        mixed = level_slope(face) if end else -level_slope(face)
        value = time_step * (near[end] + face + far[end] * mixed)
        for level in range(levels):
            fix_send[level, end : end + 1, :] = value[level : level + 1, :]

    def fix_to(level, other, sem):
        return send(fix_send.at[level], fix_recv.at[my, me], sem, fix_come, {"px": level, "py": other})

    def give_even(at, _):
        level = level_of(at, 0)

        @pl.when(level != me)
        def _():
            fix_to(level, my, fix_sent.at[level]).start()

        @pl.when(level == me)
        def _():
            pltpu.make_async_copy(fix_send.at[level], fix_recv.at[my, me], fix_come).start()

        return 0

    def give_odd(at, _):
        level = level_of(at, 1)
        for other in range(npy):
            @pl.when(level != me)
            def _():
                fix_to(level, other, fix_sent.at[level]).start()

            @pl.when((level == me) & (other != my))
            def _():
                fix_to(level, other, fix_own.at[other]).start()

            @pl.when((level == me) & (other == my))
            def _():
                pltpu.make_async_copy(fix_send.at[level], fix_recv.at[my, me], fix_come).start()

        return 0

    lax.fori_loop(0, pairs, give_even, 0)
    lax.fori_loop(0, pairs, give_odd, 0)

    order = [*range(1, npy), 0]
    turn = jnp.where(my < npy // 2, 1, npy - 1)

    def mate(step):
        return lax.rem(my + step * turn, npy)

    def whole(ref, sem):
        return pltpu.make_async_copy(ref, ref, sem)

    def narrow(value, shape):
        return value.astype(jnp.bfloat16).reshape(shape)

    def mend(ref, at, where_cols, value):
        for end in range(2):
            first = where_cols + (cols - 128) * end
            now = ref[at, :, first : first + 128].astype(jnp.float32)
            spot = lane[: now.shape[0]] == 127 * end
            ref[at, :, first : first + 128] = jnp.where(spot, value(end), now).astype(jnp.bfloat16)

    def mid_to_cross(other, source):
        return send(mid.at[other], cross.at[:, :, strip(source)], mid_send.at[other], cross_come, {"py": other})

    def mid_to_lines(other, source):
        return send(mid.at[other], lines.at[:, rows_of(source), :], mid_send.at[other], lines_come, {"py": other})

    def two_to(other_y, other_x, sem):
        return send(
            two.at[other_y, other_x], out.at[me, rows_of(my), :], sem, out_recv.at[me], {"px": other_x, "py": other_y}
        )

    def fin_to(other):
        return send(fin.at[other], out.at[me], fin_send.at[other], out_recv.at[me], {"px": other})

    def over_px(body):
        def one_step(at, _):
            body(lax.rem(me + at, npx))
            return 0

        lax.fori_loop(1, npx, one_step, 0)

    @pl.when(x_first)
    def _():
        whole(fix_recv.at[my], fix_come).wait()
        for p in range(npx):
            fix_rows[2 * p : 2 * p + 2, :] = fix_recv[my, p]
        fix_cols[...] = jnp.transpose(fix_rows[...])
        whole(lines, lines_come).wait()
        for p in range(npx):
            mend(lines, p, 0, lambda end: fix_cols[:, 2 * p + end : 2 * p + end + 1])
        loads[4].wait()
        for step in order:
            other = mate(step)
            mine = ix[:, rows_of(other), :].reshape(npx * part, order_x)
            value = jnp.dot(mine, lines[...].reshape(order_x, cols), preferred_element_type=jnp.float32)
            mid[other] = narrow(value, (npx, part, cols))
            if step:
                mid_to_cross(other, my).start()
            else:
                pltpu.make_async_copy(mid.at[my], cross.at[:, :, strip(my)], cross_come).start()
        loads[5].wait()
        whole(cross, cross_come).wait()
        for step in order:
            other = mate(step)
            value = lax.dot_general(
                cross[...].reshape(npx * part, order_y),
                iy[strip(other), :],
                (((1,), (1,)), ((), ())),
                preferred_element_type=jnp.float32,
            )
            two[other] = narrow(value, (npx, part, cols))
            if step:
                over_px(lambda other_x: two_to(other, other_x, two_send.at[other]).start())
                two_to(other, me, two_send.at[other]).start()
            else:
                over_px(lambda other_x: two_to(my, other_x, two_own.at[other_x]).start())
                pltpu.make_async_copy(two.at[my, me], out.at[me, rows_of(my), :], out_recv.at[me]).start()

    @pl.when(jnp.logical_not(x_first))
    def _():
        whole(fix_recv, fix_come).wait()
        for q in range(npy):
            for p in range(npx):
                at = 2 * (q * npx + p)
                fix_rows[at : at + 2, :] = fix_recv[q, p]
        fix_cols[...] = jnp.transpose(fix_rows[...])
        whole(cross, cross_come).wait()
        for q in range(npy):
            for p in range(npx):
                at = 2 * (q * npx + p)
                mend(cross, p, q * cols, lambda end: fix_cols[rows_of(my), at + end : at + end + 1])
        loads[5].wait()
        for step in order:
            other = mate(step)
            value = lax.dot_general(
                cross[...].reshape(npx * part, order_y),
                iy[strip(other), :],
                (((1,), (1,)), ((), ())),
                preferred_element_type=jnp.float32,
            )
            mid[other] = narrow(value, (npx, part, cols))
            if step:
                mid_to_lines(other, my).start()
            else:
                pltpu.make_async_copy(mid.at[my], lines.at[:, rows_of(my), :], lines_come).start()
        loads[4].wait()
        whole(lines, lines_come).wait()
        half = npx // pairs
        for at in range(pairs):
            first = half * lax.rem(me // half + 1 + at, pairs)
            value = jnp.dot(
                ix[pl.ds(first, half)].reshape(half * rows, order_x),
                lines[...].reshape(order_x, cols),
                preferred_element_type=jnp.float32,
            )
            fin[pl.ds(first, half)] = narrow(value, (half, rows, cols))
            for other in (first, first + 1):
                @pl.when(other != me)
                def _():
                    fin_to(other).start()

                @pl.when(other == me)
                def _():
                    pltpu.make_async_copy(fin.at[me], out.at[me], out_recv.at[me]).start()

    for halo in halos_x + halos_y:
        halo.wait_send()

    def sent(other):
        whole(rhs.at[other], rhs_send.at[other]).wait()

        @pl.when(lax.rem(other, 2) == 0)
        def _():
            whole(fix_send.at[other], fix_sent.at[other]).wait()

        @pl.when(lax.rem(other, 2) == 1)
        def _():
            whole(fix_recv.at[:, 0], fix_sent.at[other]).wait()

    over_px(sent)
    for step in range(1, npy):
        other = lax.rem(my + step, npy)
        whole(mid.at[other], mid_send.at[other]).wait()

    @pl.when(x_first)
    def _():
        for step in range(1, npy):
            other = lax.rem(my + step, npy)
            whole(two.at[other], two_send.at[other]).wait()
        over_px(lambda other: whole(two.at[my, other], two_own.at[other]).wait())

    @pl.when(jnp.logical_not(x_first))
    def _():
        for step in range(1, npy):
            other = lax.rem(my + step, npy)
            whole(rhs.at[me, rows_of(other), :], own_send.at[other]).wait()
            whole(fix_send.at[me], fix_own.at[other]).wait()
        over_px(lambda other: whole(fin.at[other], fin_send.at[other]).wait())

    def settle(level, _):
        whole(out.at[level], out_recv.at[level]).wait()
        return 0

    lax.fori_loop(0, levels, settle, 0)


def fused(velocity, forcing, cross_x, cross_y, inv_x, inv_y):
    npx, npy = lax.axis_size("px"), lax.axis_size("py")
    levels, rows, cols = velocity.shape
    part = rows // npy
    shape, narrow = velocity.shape, jnp.bfloat16
    order_x, order_y = npx * rows, npy * cols
    vmem, dma = pltpu.VMEM, pltpu.SemaphoreType.DMA
    settled = pl.pallas_call(
        functools.partial(kernel, npx, npy),
        out_shape=jax.ShapeDtypeStruct(shape, narrow),
        in_specs=[pl.BlockSpec(memory_space=pl.ANY)] * 6,
        out_specs=pl.BlockSpec(memory_space=pl.ANY),
        scratch_shapes=[
            vmem(shape, jnp.float32),
            vmem(shape, narrow),
            vmem(shape, narrow),
            vmem(shape, narrow),
            vmem((npx, rows, order_x), narrow),
            vmem((order_y, order_y), narrow),
            vmem((2, levels, cols), jnp.float32),
            vmem((2, levels, cols), jnp.float32),
            vmem((2, levels, cols), jnp.float32),
            vmem((2, levels, rows), jnp.float32),
            vmem((2, levels, rows), jnp.float32),
            vmem((levels + 2, rows, cols), jnp.float32),
            vmem((levels + 2, rows, cols), jnp.float32),
            vmem(shape, jnp.float32),
            vmem((levels, rows, cols), narrow),
            vmem((npx, rows, cols), narrow),
            vmem((npx, part, order_y), narrow),
            vmem((npy, npx, part, cols), narrow),
            vmem((npy, npx, part, cols), narrow),
            vmem((npx, rows, cols), narrow),
            vmem((levels, 2, rows), jnp.float32),
            vmem((npy, npx, 2, rows), jnp.float32),
            vmem((128, rows), jnp.float32),
            vmem((rows, 128), jnp.float32),
            dma((6,)),
            dma((4,)),
            dma((4,)),
            dma((levels,)),
            dma((npy,)),
            dma((levels,)),
            dma((npy,)),
            dma,
            dma,
            dma,
            dma((npy,)),
            dma((npy,)),
            dma((npx,)),
            dma((npx,)),
            dma((levels,)),
        ],
        compiler_params=pltpu.CompilerParams(collective_id=0, has_side_effects=True, vmem_limit_bytes=56_000_000),
        cost_estimate=pl.CostEstimate(flops=4 * order_x * order_y * rows, bytes_accessed=8 * 1024 * 1024, transcendentals=0),
    )(
        velocity,
        forcing,
        cross_x,
        cross_y,
        inv_x.reshape(npx, rows, order_x),
        inv_y.reshape(order_y, order_y),
    )
    return velocity + settled.astype(jnp.float32)


def step(velocity, forcing, cross_x, cross_y, inv_x, inv_y):
    npx, npy = lax.axis_size("px"), lax.axis_size("py")
    levels, rows, cols = velocity.shape
    aligned = rows % (32 * npy) == 0 and rows % 128 == 0 and cols % 128 == 0 and levels % 8 == 0
    paired = npx % 2 == 0 and npy > 1 and 2 * npx * npy <= 128
    if aligned and paired and levels == npx and inv_x.shape[0] == 1:
        return fused(velocity, forcing, cross_x, cross_y, inv_x, inv_y)
    return shards(velocity, forcing, cross_x, cross_y, inv_x, inv_y)


def solution(mesh):
    return jax.shard_map(
        step,
        mesh=mesh,
        in_specs=(
            P(None, "px", "py"),
            P(None, "px", "py"),
            P(None, "px", "py"),
            P(None, "px", "py"),
            P("px", None, None),
            P("px", None, None),
        ),
        out_specs=P(None, "px", "py"),
        check_vma=False,
    )
```

```python
import functools

import jax
import jax.numpy as jnp
from jax import lax
from jax.experimental import pallas as pl
from jax.experimental.pallas import tpu as pltpu
from jax.sharding import PartitionSpec as P

time_step = 0.25


def with_halo(cells, sides, width):
    for axis, dim in sides:
        count = lax.axis_size(axis)
        head = lax.slice_in_dim(cells, 0, width, axis=dim)
        tail = lax.slice_in_dim(cells, cells.shape[dim] - width, cells.shape[dim], axis=dim)
        cells = jnp.concatenate(
            [
                lax.ppermute(tail, axis, [(i, (i + 1) % count) for i in range(count)]),
                cells,
                lax.ppermute(head, axis, [((i + 1) % count, i) for i in range(count)]),
            ],
            axis=dim,
        )
    return cells


def shards(velocity, forcing, cross_x, cross_y, inv_x, inv_y):
    padded = with_halo(velocity, (("px", 1), ("py", 2)), 1)
    x_plus = padded[:, 2:, 1:-1]
    x_minus = padded[:, :-2, 1:-1]
    y_plus = padded[:, 1:-1, 2:]
    y_minus = padded[:, 1:-1, :-2]
    z_padded = jnp.pad(velocity, ((1, 1), (0, 0), (0, 0)))
    laplace = (
        x_plus
        + x_minus
        + y_plus
        + y_minus
        - 4.0 * velocity
        + z_padded[2:]
        + z_padded[:-2]
        - 2.0 * velocity
    )
    slope_x = jnp.pad(0.5 * (x_plus - x_minus), ((1, 1), (0, 0), (0, 0)))
    slope_y = jnp.pad(0.5 * (y_plus - y_minus), ((1, 1), (0, 0), (0, 0)))
    mixed_x = 0.5 * (slope_x[2:] - slope_x[:-2])
    mixed_y = 0.5 * (slope_y[2:] - slope_y[:-2])
    total = (
        laplace
        + cross_x.astype(jnp.float32) * mixed_x
        + cross_y.astype(jnp.float32) * mixed_y
        + forcing.astype(jnp.float32)
    )
    rhs = (time_step * total).astype(jnp.bfloat16)
    section_one = jnp.einsum(
        "lab,lbk->lak",
        inv_x,
        lax.all_to_all(rhs, "px", split_axis=0, concat_axis=1, tiled=True),
        preferred_element_type=jnp.float32,
    ).astype(jnp.bfloat16)
    y_lines = lax.all_to_all(section_one, "py", split_axis=1, concat_axis=2, tiled=True)
    section_two = jnp.einsum("lxb,lab->lxa", y_lines, inv_y, preferred_element_type=jnp.float32)
    settled = lax.all_to_all(
        lax.all_to_all(section_two, "py", split_axis=2, concat_axis=1, tiled=True),
        "px",
        split_axis=1,
        concat_axis=0,
        tiled=True,
    )
    return velocity + settled


def send(src, dst, send_sem, recv_sem, target):
    return pltpu.make_async_remote_copy(
        src_ref=src,
        dst_ref=dst,
        send_sem=send_sem,
        recv_sem=recv_sem,
        device_id=target,
        device_id_type=pl.DeviceIdType.MESH,
    )


def kernel(
    npx,
    npy,
    vel_hbm,
    frc_hbm,
    cx_hbm,
    cy_hbm,
    ix_hbm,
    iy_hbm,
    out,
    vel,
    frc,
    cx,
    cy,
    ix,
    iy,
    x_send,
    x_recv,
    cx_ends,
    y_send,
    y_recv,
    cy_ends,
    rhs,
    lines,
    relay,
    cross,
    mid,
    two,
    fin,
    fix_send,
    fix_recv,
    fix_rows,
    fix_cols,
    load_sem,
    halo_send,
    halo_recv,
    rhs_send,
    own_send,
    fix_sent,
    fix_come,
    lines_come,
    relay_come,
    cross_come,
    pass_send,
    ready,
    mid_send,
    two_send,
    two_own,
    fin_send,
    out_recv,
):
    me = lax.axis_index("px")
    my = lax.axis_index("py")
    levels, rows, cols = vel.shape
    part = rows // npy
    order_x, order_y = npx * rows, npy * cols
    x_first = lax.rem(me, 2) == 0
    pieces = [(vel_hbm, vel), (frc_hbm, frc), (cx_hbm, cx), (cy_hbm, cy), (ix_hbm, ix), (iy_hbm, iy)]
    loads = [pltpu.make_async_copy(a, b, load_sem.at[i]) for i, (a, b) in enumerate(pieces)]
    for load in loads:
        load.start()

    barrier = pltpu.get_barrier_semaphore()

    def greet(where):
        pl.semaphore_signal(barrier, inc=1, device_id=where, device_id_type=pl.DeviceIdType.MESH)

    twin = me + 1 - 2 * lax.rem(me, 2)
    for step in range(1, npy):
        other = lax.rem(my + step, npy)
        greet({"py": other})
        greet({"px": twin, "py": other})
    for step in range(1, npx):
        greet({"px": lax.rem(me + step, npx)})
    fix_rows[...] = jnp.zeros_like(fix_rows)
    loads[0].wait()
    lane = lax.broadcasted_iota(jnp.int32, (rows, 128), 1)
    zero = jnp.zeros((rows, 128), jnp.float32)

    for level in range(levels):
        x_send[0, level : level + 1, :] = vel[level, 0:1, :]
        x_send[1, level : level + 1, :] = vel[level, rows - 1 : rows, :]
    first, last = zero, zero
    for level in range(levels):
        first = jnp.where(lane == level, vel[level, :, 0:1], first)
        last = jnp.where(lane == level, vel[level, :, cols - 1 : cols], last)
    y_send[0], y_send[1] = jnp.transpose(first)[:levels], jnp.transpose(last)[:levels]
    pl.semaphore_wait(barrier, npx - 1 + 2 * (npy - 1))

    up_x, down_x = lax.rem(me + 1, npx), lax.rem(me + npx - 1, npx)
    up_y, down_y = lax.rem(my + 1, npy), lax.rem(my + npy - 1, npy)
    halos_y = [
        send(y_send.at[1], y_recv.at[0], halo_send.at[0], halo_recv.at[0], {"py": up_y}),
        send(y_send.at[0], y_recv.at[1], halo_send.at[1], halo_recv.at[1], {"py": down_y}),
    ]
    halos_x = [
        send(x_send.at[1], x_recv.at[0], halo_send.at[2], halo_recv.at[2], {"px": up_x}),
        send(x_send.at[0], x_recv.at[1], halo_send.at[3], halo_recv.at[3], {"px": down_x}),
    ]
    for halo in halos_y + halos_x:
        halo.start()
    for step in range(2, npy - 1):
        pl.semaphore_signal(
            ready, inc=1, device_id={"py": lax.rem(my + step, npy)}, device_id_type=pl.DeviceIdType.MESH
        )
    for load in loads[1:4]:
        load.wait()

    def strip(at):
        return pl.ds(pl.multiple_of(at * cols, cols), cols)

    def rows_of(at):
        return pl.ds(pl.multiple_of(at * part, part), part)

    def inner(level):
        now = vel[level]
        above = jnp.where(level < levels - 1, 1.0, 0.0) * vel[jnp.minimum(level + 1, levels - 1)]
        below = jnp.where(level > 0, 1.0, 0.0) * vel[jnp.maximum(level - 1, 0)]
        rise = above - below
        total = pltpu.roll(now, 1, 0) + pltpu.roll(now, rows - 1, 0) + pltpu.roll(now, 1, 1) + pltpu.roll(now, cols - 1, 1)
        total += above + below - 6.0 * now + frc[level].astype(jnp.float32)
        total += cx[level].astype(jnp.float32) * (0.25 * (pltpu.roll(rise, rows - 1, 0) - pltpu.roll(rise, 1, 0)))
        total += cy[level].astype(jnp.float32) * (0.25 * (pltpu.roll(rise, cols - 1, 1) - pltpu.roll(rise, 1, 1)))
        rhs[level] = (time_step * total).astype(jnp.bfloat16)

    def to_cross(level, other):
        src, dst = rhs.at[level, rows_of(other), :], cross.at[me, :, strip(my)]

        def away(sem):
            return send(src, dst, sem, cross_come, {"px": level, "py": other})

        @pl.when(level != me)
        def _():
            away(rhs_send.at[level]).start()

        @pl.when((level == me) & (other != my))
        def _():
            away(own_send.at[other]).start()

        @pl.when((level == me) & (other == my))
        def _():
            pltpu.make_async_copy(src, dst, cross_come).start()

    def to_relay(at, level, other):
        send(
            rhs.at[level, rows_of(other), :],
            relay.at[lax.rem(me, 2), my, at],
            rhs_send.at[level],
            relay_come.at[lax.rem(me, 2), my, at],
            {"px": 2 * (me // 2) + 1, "py": other},
        ).start()

    turn = jnp.where(my < npy // 2, 1, npy - 1)

    def mate(step):
        return lax.rem(my + step * turn, npy)

    def to_lines(level):
        @pl.when(level != me)
        def _():
            send(rhs.at[level], lines.at[me], rhs_send.at[level], lines_come, {"px": level}).start()

        @pl.when(level == me)
        def _():
            pltpu.make_async_copy(rhs.at[level], lines.at[me], lines_come).start()

    pairs = npx // 2

    def level_of(at, odd):
        return 2 * lax.rem(me // 2 + 1 + at, pairs) + odd

    here = level_of(pairs - 1, 1)

    def one_pair(at, _):
        odd = level_of(at, 1)
        inner(odd)
        for step in range(npy - 1, 0, -1):
            to_relay(at, odd, mate(step))
        even = level_of(at, 0)
        inner(even)
        to_lines(even)
        return 0

    def near_odd(at, _):
        to_cross(level_of(at, 1), my)
        return 0

    lax.fori_loop(0, pairs - 1, one_pair, 0)
    inner(here)
    for step in range(npy - 1, -1, -1):
        to_cross(here, mate(step))
    inner(here - 1)
    to_lines(here - 1)
    lax.fori_loop(0, pairs - 1, near_odd, 0)
    def level_slope(face):
        at = lax.broadcasted_iota(jnp.int32, face.shape, 0)
        lower = jnp.where(at == 0, 0.0, pltpu.roll(face, 1, 0))
        upper = jnp.where(at == levels - 1, 0.0, pltpu.roll(face, levels - 1, 0))
        return 0.25 * (upper - lower)

    pick_row = lax.broadcasted_iota(jnp.int32, (16, cols), 0)
    pick_col = lax.broadcasted_iota(jnp.int32, (16, cols), 1)
    pick = ((pick_row == 0) & (pick_col == 0)) | ((pick_row == 1) & (pick_col == cols - 1))
    picked = lax.dot_general(
        pick.astype(jnp.bfloat16), cy[...].reshape(levels * rows, cols), (((1,), (1,)), ((), ())), preferred_element_type=jnp.float32
    )
    for end in range(2):
        for level in range(levels):
            cy_ends[end, level : level + 1, :] = picked[end : end + 1, level * rows : (level + 1) * rows]
    for level in range(levels):
        cx_ends[0, level : level + 1, :] = cx[level, 0:16, :].astype(jnp.float32)[0:1]
        cx_ends[1, level : level + 1, :] = cx[level, rows - 16 : rows, :].astype(jnp.float32)[15:16]

    def correct(end, came, gone, metric, lanes):
        face = came[end] - gone[1 - end]
        mixed = level_slope(face) if end else -level_slope(face)
        value = time_step * (face + metric[end] * mixed)
        for level in range(levels):
            fix_send[level, end : end + 1, lanes] = value[level : level + 1, :]

    for halo in halos_x:
        halo.wait_recv()
    for end in range(2):
        correct(end, x_recv, x_send, cx_ends, slice(rows, rows + cols))
    for halo in halos_y:
        halo.wait_recv()
    for end in range(2):
        correct(end, y_recv, y_send, cy_ends, slice(0, rows))
    if npy > 3:
        pl.semaphore_wait(ready, npy - 3)

    def fix_to(level, other, sem, lanes):
        return send(
            fix_send.at[level, :, pl.ds(0, lanes)],
            fix_recv.at[my, me, :, pl.ds(0, lanes)],
            sem,
            fix_come,
            {"px": level, "py": other},
        )

    def fix_here(level, lanes):
        pltpu.make_async_copy(
            fix_send.at[level, :, pl.ds(0, lanes)], fix_recv.at[my, me, :, pl.ds(0, lanes)], fix_come
        ).start()

    def give_even(at, _):
        level = level_of(at, 0)

        @pl.when(level != me)
        def _():
            fix_to(level, my, fix_sent.at[level, my], rows + cols).start()

        @pl.when(level == me)
        def _():
            fix_here(level, rows + cols)

        return 0

    def fix_lanes(other):
        return rows + cols if other in (0, npy - 1) else rows

    def give_odd(at, _):
        level = level_of(at, 1)
        for other in range(npy):
            mine = (level == me) & (other == my)

            @pl.when(jnp.logical_not(mine))
            def _():
                fix_to(level, other, fix_sent.at[level, other], fix_lanes(other)).start()

            @pl.when(mine)
            def _():
                fix_here(level, fix_lanes(other))

        return 0

    lax.fori_loop(0, pairs, give_even, 0)
    lax.fori_loop(0, pairs, give_odd, 0)

    order = [*range(npy - 1, 0, -1), 0]
    def whole(ref, sem):
        return pltpu.make_async_copy(ref, ref, sem)

    def narrow(value, shape):
        return value.astype(jnp.bfloat16).reshape(shape)

    def mend(ref, at, where_cols, value):
        for end in range(2):
            first = where_cols + (cols - 128) * end
            now = ref[at, :, first : first + 128].astype(jnp.float32)
            spot = lane[: now.shape[0]] == 127 * end
            ref[at, :, first : first + 128] = (now + jnp.where(spot, value(end), 0.0)).astype(jnp.bfloat16)

    def mend_row(ref, at, first, end, where_cols, value):
        spot = lax.broadcasted_iota(jnp.int32, (16, cols), 0) == 15 * end
        block = (at, slice(first, first + 16), slice(where_cols, where_cols + cols))
        ref[block] = (ref[block].astype(jnp.float32) + jnp.where(spot, value, 0.0)).astype(jnp.bfloat16)

    def mid_to_cross(other, source):
        return send(mid.at[other], cross.at[:, :, strip(source)], mid_send.at[other], cross_come, {"py": other})

    def mid_to_lines(other, source):
        return send(mid.at[other], lines.at[:, rows_of(source), :], mid_send.at[other], lines_come, {"py": other})

    def pass_on(at, core, source):
        spot = (core, source, at)
        whole(relay.at[spot], relay_come.at[spot]).wait()
        send(
            relay.at[spot],
            cross.at[2 * (me // 2) + core, :, strip(source)],
            pass_send.at[core, source],
            cross_come,
            {"px": level_of(at, 1)},
        ).start()

    def two_to(other_y, other_x, sem):
        return send(
            two.at[other_y, other_x], out.at[me, rows_of(my), :], sem, out_recv.at[me], {"px": other_x, "py": other_y}
        )

    def fin_to(other):
        return send(fin.at[other], out.at[me], fin_send.at[other], out_recv.at[me], {"px": other})

    def over_px(body):
        def one_step(at, _):
            body(lax.rem(me + at, npx))
            return 0

        lax.fori_loop(1, npx, one_step, 0)

    @pl.when(x_first)
    def _():
        whole(lines, lines_come).wait()
        whole(fix_recv.at[my], fix_come).wait()
        for p in range(npx):
            fix_rows[2 * p : 2 * p + 2, :] = fix_recv[my, p, :, 0:rows]
        fix_cols[...] = jnp.transpose(fix_rows[...])
        for p in range(npx):
            mend(lines, p, 0, lambda end: fix_cols[:, 2 * p + end : 2 * p + end + 1])
            for end in range(2):
                mend_row(lines, p, (rows - 16) * end, end, 0, fix_recv[my, p, end : end + 1, rows : rows + cols])
        loads[4].wait()
        for step in order:
            other = mate(step)
            mine = ix[:, rows_of(other), :].reshape(npx * part, order_x)
            value = jnp.dot(mine, lines[...].reshape(order_x, cols), preferred_element_type=jnp.float32)
            mid[other] = narrow(value, (npx, part, cols))
            if step:
                mid_to_cross(other, my).start()
            else:
                pltpu.make_async_copy(mid.at[my], cross.at[:, :, strip(my)], cross_come).start()
        loads[5].wait()
        whole(cross, cross_come).wait()
        for step in order:
            other = mate(step)
            value = lax.dot_general(
                cross[...].reshape(npx * part, order_y),
                iy[strip(other), :],
                (((1,), (1,)), ((), ())),
                preferred_element_type=jnp.float32,
            )
            two[other] = narrow(value, (npx, part, cols))
            if step:
                over_px(lambda other_x: two_to(other, other_x, two_send.at[other]).start())
                two_to(other, me, two_send.at[other]).start()
            else:
                over_px(lambda other_x: two_to(my, other_x, two_own.at[other_x]).start())
                pltpu.make_async_copy(two.at[my, me], out.at[me, rows_of(my), :], out_recv.at[me]).start()

    @pl.when(jnp.logical_not(x_first))
    def _():
        def pass_level(at, _):
            for step in range(1, npy):
                for core in range(2):
                    pass_on(at, core, mate(step))
            return 0

        lax.fori_loop(0, pairs - 1, pass_level, 0)
        whole(cross, cross_come).wait()
        outer = (my == 0) | (my == npy - 1)

        @pl.when(outer)
        def _():
            whole(fix_recv, fix_come).wait()

        @pl.when(jnp.logical_not(outer))
        def _():
            whole(fix_recv.at[:, :, :, pl.ds(0, rows)], fix_come).wait()

        for q in range(npy):
            for p in range(npx):
                at = 2 * (q * npx + p)
                fix_rows[at : at + 2, :] = fix_recv[q, p, :, 0:rows]
        fix_cols[...] = jnp.transpose(fix_rows[...])
        for q in range(npy):
            for p in range(npx):
                at = 2 * (q * npx + p)
                mend(cross, p, q * cols, lambda end: fix_cols[rows_of(my), at + end : at + end + 1])
        for end in range(2):
            @pl.when(my == (npy - 1) * end)
            def _():
                for q in range(npy):
                    for p in range(npx):
                        value = fix_recv[q, p, end : end + 1, rows : rows + cols]
                        mend_row(cross, p, (part - 16) * end, end, q * cols, value)

        loads[5].wait()
        for step in order:
            other = mate(step)
            value = lax.dot_general(
                cross[...].reshape(npx * part, order_y),
                iy[strip(other), :],
                (((1,), (1,)), ((), ())),
                preferred_element_type=jnp.float32,
            )
            mid[other] = narrow(value, (npx, part, cols))
            if step:
                mid_to_lines(other, my).start()
            else:
                pltpu.make_async_copy(mid.at[my], lines.at[:, rows_of(my), :], lines_come).start()
        loads[4].wait()
        whole(lines, lines_come).wait()
        half = npx // pairs
        for at in range(pairs):
            first = half * lax.rem(me // half + 1 + at, pairs)
            value = jnp.dot(
                ix[pl.ds(first, half)].reshape(half * rows, order_x),
                lines[...].reshape(order_x, cols),
                preferred_element_type=jnp.float32,
            )
            fin[pl.ds(first, half)] = narrow(value, (half, rows, cols))
            for other in (first, first + 1):
                @pl.when(other != me)
                def _():
                    fin_to(other).start()

                @pl.when(other == me)
                def _():
                    pltpu.make_async_copy(fin.at[me], out.at[me], out_recv.at[me]).start()

    for halo in halos_x + halos_y:
        halo.wait_send()

    def sent(other):
        whole(rhs.at[other], rhs_send.at[other]).wait()

        @pl.when(lax.rem(other, 2) == 0)
        def _():
            fix_to(other, my, fix_sent.at[other, my], rows + cols).wait_send()

        @pl.when(lax.rem(other, 2) == 1)
        def _():
            for plane in range(npy):
                fix_to(other, plane, fix_sent.at[other, plane], fix_lanes(plane)).wait_send()

    over_px(sent)
    for step in range(1, npy):
        other = lax.rem(my + step, npy)
        whole(mid.at[other], mid_send.at[other]).wait()

    @pl.when(x_first)
    def _():
        for step in range(1, npy):
            other = lax.rem(my + step, npy)
            whole(two.at[other], two_send.at[other]).wait()
        over_px(lambda other: whole(two.at[my, other], two_own.at[other]).wait())

    @pl.when(jnp.logical_not(x_first))
    def _():
        for step in range(1, npy):
            other = lax.rem(my + step, npy)
            whole(rhs.at[me, rows_of(other), :], own_send.at[other]).wait()
            for core in range(2):
                whole(relay.at[core, other], pass_send.at[core, other]).wait()
        for plane in range(npy):
            @pl.when(plane != my)
            def _():
                fix_to(me, plane, fix_sent.at[me, plane], fix_lanes(plane)).wait_send()

        over_px(lambda other: whole(fin.at[other], fin_send.at[other]).wait())

    def settle(level, _):
        whole(out.at[level], out_recv.at[level]).wait()
        return 0

    lax.fori_loop(0, levels, settle, 0)


def fused(velocity, forcing, cross_x, cross_y, inv_x, inv_y):
    npx, npy = lax.axis_size("px"), lax.axis_size("py")
    levels, rows, cols = velocity.shape
    part = rows // npy
    shape, narrow = velocity.shape, jnp.bfloat16
    order_x, order_y = npx * rows, npy * cols
    vmem, dma = pltpu.VMEM, pltpu.SemaphoreType.DMA
    settled = pl.pallas_call(
        functools.partial(kernel, npx, npy),
        out_shape=jax.ShapeDtypeStruct(shape, narrow),
        in_specs=[pl.BlockSpec(memory_space=pl.ANY)] * 6,
        out_specs=pl.BlockSpec(memory_space=pl.ANY),
        scratch_shapes=[
            vmem(shape, jnp.float32),
            vmem(shape, narrow),
            vmem(shape, narrow),
            vmem(shape, narrow),
            vmem((npx, rows, order_x), narrow),
            vmem((order_y, order_y), narrow),
            vmem((2, levels, cols), jnp.float32),
            vmem((2, levels, cols), jnp.float32),
            vmem((2, levels, cols), jnp.float32),
            vmem((2, levels, rows), jnp.float32),
            vmem((2, levels, rows), jnp.float32),
            vmem((2, levels, rows), jnp.float32),
            vmem((levels, rows, cols), narrow),
            vmem((npx, rows, cols), narrow),
            vmem((2, npy, max(npx // 2 - 1, 1), part, cols), narrow),
            vmem((npx, part, order_y), narrow),
            vmem((npy, npx, part, cols), narrow),
            vmem((npy, npx, part, cols), narrow),
            vmem((npx, rows, cols), narrow),
            vmem((levels, 2, rows + cols), jnp.float32),
            vmem((npy, npx, 2, rows + cols), jnp.float32),
            vmem((128, rows), jnp.float32),
            vmem((rows, 128), jnp.float32),
            dma((6,)),
            dma((4,)),
            dma((4,)),
            dma((levels,)),
            dma((npy,)),
            dma((levels, npy)),
            dma,
            dma,
            dma((2, npy, max(npx // 2 - 1, 1))),
            dma,
            dma((2, npy)),
            pltpu.SemaphoreType.REGULAR,
            dma((npy,)),
            dma((npy,)),
            dma((npx,)),
            dma((npx,)),
            dma((levels,)),
        ],
        compiler_params=pltpu.CompilerParams(collective_id=0, has_side_effects=True, vmem_limit_bytes=56_000_000),
        cost_estimate=pl.CostEstimate(flops=4 * order_x * order_y * rows, bytes_accessed=8 * 1024 * 1024, transcendentals=0),
    )(
        velocity,
        forcing,
        cross_x,
        cross_y,
        inv_x.reshape(npx, rows, order_x),
        inv_y.reshape(order_y, order_y),
    )
    return velocity + settled.astype(jnp.float32)


def step(velocity, forcing, cross_x, cross_y, inv_x, inv_y):
    npx, npy = lax.axis_size("px"), lax.axis_size("py")
    levels, rows, cols = velocity.shape
    aligned = rows % (32 * npy) == 0 and rows % 128 == 0 and cols % 128 == 0 and levels % 8 == 0
    paired = npx % 2 == 0 and npx > 2 and npy > 1 and 2 * npx * npy <= 128
    if aligned and paired and levels == npx and inv_x.shape[0] == 1:
        return fused(velocity, forcing, cross_x, cross_y, inv_x, inv_y)
    return shards(velocity, forcing, cross_x, cross_y, inv_x, inv_y)


def solution(mesh):
    return jax.shard_map(
        step,
        mesh=mesh,
        in_specs=(
            P(None, "px", "py"),
            P(None, "px", "py"),
            P(None, "px", "py"),
            P(None, "px", "py"),
            P("px", None, None),
            P("px", None, None),
        ),
        out_specs=P(None, "px", "py"),
        check_vma=False,
    )
```

```python
import functools

import jax
import jax.numpy as jnp
from jax import lax
from jax.experimental import pallas as pl
from jax.experimental.pallas import tpu as pltpu
from jax.sharding import PartitionSpec as P

time_step = 0.25


def with_halo(cells, sides, width):
    for axis, dim in sides:
        count = lax.axis_size(axis)
        head = lax.slice_in_dim(cells, 0, width, axis=dim)
        tail = lax.slice_in_dim(cells, cells.shape[dim] - width, cells.shape[dim], axis=dim)
        cells = jnp.concatenate(
            [
                lax.ppermute(tail, axis, [(i, (i + 1) % count) for i in range(count)]),
                cells,
                lax.ppermute(head, axis, [((i + 1) % count, i) for i in range(count)]),
            ],
            axis=dim,
        )
    return cells


def shards(velocity, forcing, cross_x, cross_y, inv_x, inv_y):
    padded = with_halo(velocity, (("px", 1), ("py", 2)), 1)
    x_plus = padded[:, 2:, 1:-1]
    x_minus = padded[:, :-2, 1:-1]
    y_plus = padded[:, 1:-1, 2:]
    y_minus = padded[:, 1:-1, :-2]
    z_padded = jnp.pad(velocity, ((1, 1), (0, 0), (0, 0)))
    laplace = (
        x_plus
        + x_minus
        + y_plus
        + y_minus
        - 4.0 * velocity
        + z_padded[2:]
        + z_padded[:-2]
        - 2.0 * velocity
    )
    slope_x = jnp.pad(0.5 * (x_plus - x_minus), ((1, 1), (0, 0), (0, 0)))
    slope_y = jnp.pad(0.5 * (y_plus - y_minus), ((1, 1), (0, 0), (0, 0)))
    mixed_x = 0.5 * (slope_x[2:] - slope_x[:-2])
    mixed_y = 0.5 * (slope_y[2:] - slope_y[:-2])
    total = (
        laplace
        + cross_x.astype(jnp.float32) * mixed_x
        + cross_y.astype(jnp.float32) * mixed_y
        + forcing.astype(jnp.float32)
    )
    rhs = (time_step * total).astype(jnp.bfloat16)
    section_one = jnp.einsum(
        "lab,lbk->lak",
        inv_x,
        lax.all_to_all(rhs, "px", split_axis=0, concat_axis=1, tiled=True),
        preferred_element_type=jnp.float32,
    ).astype(jnp.bfloat16)
    y_lines = lax.all_to_all(section_one, "py", split_axis=1, concat_axis=2, tiled=True)
    section_two = jnp.einsum("lxb,lab->lxa", y_lines, inv_y, preferred_element_type=jnp.float32)
    settled = lax.all_to_all(
        lax.all_to_all(section_two, "py", split_axis=2, concat_axis=1, tiled=True),
        "px",
        split_axis=1,
        concat_axis=0,
        tiled=True,
    )
    return velocity + settled


def send(src, dst, send_sem, recv_sem, target):
    return pltpu.make_async_remote_copy(
        src_ref=src,
        dst_ref=dst,
        send_sem=send_sem,
        recv_sem=recv_sem,
        device_id=target,
        device_id_type=pl.DeviceIdType.MESH,
    )


def kernel(
    npx,
    npy,
    vel_hbm,
    frc_hbm,
    cx_hbm,
    cy_hbm,
    ix_hbm,
    iy_hbm,
    out,
    vel,
    frc,
    cx,
    cy,
    ix,
    iy,
    x_send,
    x_recv,
    cx_ends,
    y_send,
    y_recv,
    cy_ends,
    rhs,
    lines,
    relay,
    cross,
    mid,
    two,
    fin,
    fix_send,
    fix_recv,
    fix_rows,
    fix_cols,
    load_sem,
    relay_come,
    x_sent,
    x_come,
    y_sent,
    y_come,
    rhs_send,
    own_send,
    fix_sent,
    fix_come,
    lines_come,
    cross_come,
    pass_send,
    mid_send,
    last_send,
    out_recv,
    ready,
    gate,
):
    me = lax.axis_index("px")
    my = lax.axis_index("py")
    levels, rows, cols = vel.shape
    part = rows // npy
    order_x, order_y = npx * rows, npy * cols
    x_first = lax.rem(me, 2) == 0
    pieces = [(vel_hbm, vel), (frc_hbm, frc), (cx_hbm, cx), (cy_hbm, cy), (ix_hbm, ix), (iy_hbm, iy)]
    loads = [pltpu.make_async_copy(a, b, load_sem.at[i]) for i, (a, b) in enumerate(pieces)]
    for load in loads:
        load.start()

    def whole(ref, sem):
        return pltpu.make_async_copy(ref, ref, sem)

    barrier = pltpu.get_barrier_semaphore()

    def greet(where):
        pl.semaphore_signal(barrier, inc=1, device_id=where, device_id_type=pl.DeviceIdType.MESH)

    twin = me + 1 - 2 * lax.rem(me, 2)
    for step in range(1, npy):
        other = lax.rem(my + step, npy)
        greet({"py": other})
        greet({"px": twin, "py": other})
    for step in range(1, npx):
        greet({"px": lax.rem(me + step, npx)})
    fix_rows[...] = jnp.zeros_like(fix_rows)
    loads[0].wait()
    lane = lax.broadcasted_iota(jnp.int32, (rows, 128), 1)
    zero = jnp.zeros((rows, 128), jnp.float32)

    for level in range(levels):
        x_send[0, level : level + 1, :] = vel[level, 0:1, :]
        x_send[1, level : level + 1, :] = vel[level, rows - 1 : rows, :]
    first, last = zero, zero
    for level in range(levels):
        first = jnp.where(lane == level, vel[level, :, 0:1], first)
        last = jnp.where(lane == level, vel[level, :, cols - 1 : cols], last)
    y_send[0], y_send[1] = jnp.transpose(first)[:levels], jnp.transpose(last)[:levels]
    pl.semaphore_wait(barrier, npx - 1 + 2 * (npy - 1))

    up_x, down_x = lax.rem(me + 1, npx), lax.rem(me + npx - 1, npx)
    up_y, down_y = lax.rem(my + 1, npy), lax.rem(my + npy - 1, npy)
    halos_y = [
        send(y_send.at[1], y_recv.at[0], y_sent, y_come, {"py": up_y}),
        send(y_send.at[0], y_recv.at[1], y_sent, y_come, {"py": down_y}),
    ]
    halos_x = [
        send(x_send.at[1], x_recv.at[0], x_sent, x_come, {"px": up_x}),
        send(x_send.at[0], x_recv.at[1], x_sent, x_come, {"px": down_x}),
    ]
    for halo in halos_y + halos_x:
        halo.start()
    for step in range(2, npy - 1):
        pl.semaphore_signal(
            ready, inc=1, device_id={"py": lax.rem(my + step, npy)}, device_id_type=pl.DeviceIdType.MESH
        )
    for load in loads[1:4]:
        load.wait()

    def strip(at):
        return pl.ds(pl.multiple_of(at * cols, cols), cols)

    def rows_of(at):
        return pl.ds(pl.multiple_of(at * part, part), part)

    def inner(level):
        now = vel[level]
        above = jnp.where(level < levels - 1, 1.0, 0.0) * vel[jnp.minimum(level + 1, levels - 1)]
        below = jnp.where(level > 0, 1.0, 0.0) * vel[jnp.maximum(level - 1, 0)]
        rise = above - below
        total = pltpu.roll(now, 1, 0) + pltpu.roll(now, rows - 1, 0) + pltpu.roll(now, 1, 1) + pltpu.roll(now, cols - 1, 1)
        total += above + below - 6.0 * now + frc[level].astype(jnp.float32)
        total += cx[level].astype(jnp.float32) * (0.25 * (pltpu.roll(rise, rows - 1, 0) - pltpu.roll(rise, 1, 0)))
        total += cy[level].astype(jnp.float32) * (0.25 * (pltpu.roll(rise, cols - 1, 1) - pltpu.roll(rise, 1, 1)))
        rhs[level] = (time_step * total).astype(jnp.bfloat16)

    def to_cross(level, other):
        src, dst = rhs.at[level, rows_of(other), :], cross.at[me, :, strip(my)]

        def away(sem):
            return send(src, dst, sem, cross_come, {"px": level, "py": other})

        @pl.when(level != me)
        def _():
            away(rhs_send).start()

        @pl.when((level == me) & (other != my))
        def _():
            away(own_send).start()

        @pl.when((level == me) & (other == my))
        def _():
            pltpu.make_async_copy(src, dst, cross_come).start()

    def gap(source, target):
        return lax.rem(source - target + npy, npy) - 1

    def to_relay(at, level, other):
        send(
            rhs.at[level, rows_of(other), :],
            relay.at[at, gap(my, other), lax.rem(me, 2)],
            rhs_send,
            relay_come.at[at],
            {"px": 2 * (me // 2) + 1, "py": other},
        ).start()

    turn = jnp.where(my < npy // 2, 1, npy - 1)

    def mate(step):
        return lax.rem(my + step * turn, npy)

    def to_lines(level):
        @pl.when(level != me)
        def _():
            send(rhs.at[level], lines.at[me], rhs_send, lines_come, {"px": level}).start()

        @pl.when(level == me)
        def _():
            pltpu.make_async_copy(rhs.at[level], lines.at[me], lines_come).start()

    pairs = npx // 2

    def level_of(at, odd):
        return 2 * lax.rem(me // 2 + 1 + at, pairs) + odd

    here = level_of(pairs - 1, 1)

    def one_pair(at, _):
        odd = level_of(at, 1)
        inner(odd)
        for step in range(npy - 1, 0, -1):
            to_relay(at, odd, mate(step))
        even = level_of(at, 0)
        inner(even)
        to_lines(even)
        return 0

    def near_odd(at, _):
        to_cross(level_of(at, 1), my)
        return 0

    lax.fori_loop(0, pairs - 1, one_pair, 0)
    inner(here)
    for step in range(npy - 1, -1, -1):
        to_cross(here, mate(step))
    inner(here - 1)
    to_lines(here - 1)
    lax.fori_loop(0, pairs - 1, near_odd, 0)
    def level_slope(face):
        at = lax.broadcasted_iota(jnp.int32, face.shape, 0)
        lower = jnp.where(at == 0, 0.0, pltpu.roll(face, 1, 0))
        upper = jnp.where(at == levels - 1, 0.0, pltpu.roll(face, levels - 1, 0))
        return 0.25 * (upper - lower)

    pick_row = lax.broadcasted_iota(jnp.int32, (16, cols), 0)
    pick_col = lax.broadcasted_iota(jnp.int32, (16, cols), 1)
    pick = ((pick_row == 0) & (pick_col == 0)) | ((pick_row == 1) & (pick_col == cols - 1))
    picked = lax.dot_general(
        pick.astype(jnp.bfloat16), cy[...].reshape(levels * rows, cols), (((1,), (1,)), ((), ())), preferred_element_type=jnp.float32
    )
    for end in range(2):
        for level in range(levels):
            cy_ends[end, level : level + 1, :] = picked[end : end + 1, level * rows : (level + 1) * rows]
    for level in range(levels):
        cx_ends[0, level : level + 1, :] = cx[level, 0:16, :].astype(jnp.float32)[0:1]
        cx_ends[1, level : level + 1, :] = cx[level, rows - 16 : rows, :].astype(jnp.float32)[15:16]

    def correct(end, came, gone, metric, lanes):
        face = came[end] - gone[1 - end]
        mixed = level_slope(face) if end else -level_slope(face)
        value = time_step * (face + metric[end] * mixed)
        for level in range(levels):
            fix_send[level, end : end + 1, lanes] = value[level : level + 1, :]

    whole(x_recv, x_come).wait()
    for end in range(2):
        correct(end, x_recv, x_send, cx_ends, slice(rows, rows + cols))
    whole(y_recv, y_come).wait()
    for end in range(2):
        correct(end, y_recv, y_send, cy_ends, slice(0, rows))
    if npy > 3:
        pl.semaphore_wait(ready, npy - 3)

    def fix_to(level, other, sem, lanes):
        return send(
            fix_send.at[level, :, pl.ds(0, lanes)],
            fix_recv.at[my, me, :, pl.ds(0, lanes)],
            sem,
            fix_come,
            {"px": level, "py": other},
        )

    def fix_here(level, lanes):
        pltpu.make_async_copy(
            fix_send.at[level, :, pl.ds(0, lanes)], fix_recv.at[my, me, :, pl.ds(0, lanes)], fix_come
        ).start()

    def give_even(at, _):
        level = level_of(at, 0)

        @pl.when(level != me)
        def _():
            fix_to(level, my, fix_sent, rows + cols).start()

        @pl.when(level == me)
        def _():
            fix_here(level, rows + cols)

        return 0

    def fix_lanes(other):
        return rows + cols if other in (0, npy - 1) else rows

    def give_odd(at, _):
        level = level_of(at, 1)
        for other in range(npy):
            mine = (level == me) & (other == my)

            @pl.when(jnp.logical_not(mine))
            def _():
                fix_to(level, other, fix_sent, fix_lanes(other)).start()

            @pl.when(mine)
            def _():
                fix_here(level, fix_lanes(other))

        return 0

    lax.fori_loop(0, pairs, give_even, 0)
    lax.fori_loop(0, pairs, give_odd, 0)

    order = [*range(1, npy), 0]
    def narrow(value, shape):
        return value.astype(jnp.bfloat16).reshape(shape)

    def mend(ref, at, where_cols, value):
        for end in range(2):
            first = where_cols + (cols - 128) * end
            now = ref[at, :, first : first + 128].astype(jnp.float32)
            spot = lane[: now.shape[0]] == 127 * end
            ref[at, :, first : first + 128] = (now + jnp.where(spot, value(end), 0.0)).astype(jnp.bfloat16)

    def mend_row(ref, at, first, end, where_cols, value):
        spot = lax.broadcasted_iota(jnp.int32, (16, cols), 0) == 15 * end
        block = (at, slice(first, first + 16), slice(where_cols, where_cols + cols))
        ref[block] = (ref[block].astype(jnp.float32) + jnp.where(spot, value, 0.0)).astype(jnp.bfloat16)

    def mid_to_cross(other, source):
        return send(mid.at[other], cross.at[:, :, strip(source)], mid_send, cross_come, {"py": other})

    def mid_to_lines(other, source):
        return send(mid.at[other], lines.at[:, rows_of(source), :], mid_send, lines_come, {"py": other})

    def pass_on(at, core, source):
        send(
            relay.at[at, gap(source, my), core],
            cross.at[2 * (me // 2) + core, :, strip(source)],
            pass_send,
            cross_come,
            {"px": level_of(at, 1)},
        ).start()

    def two_to(other_y, other_x, sem):
        return send(
            two.at[other_y * npx + other_x], out.at[me, rows_of(my), :], sem, out_recv, {"px": other_x, "py": other_y}
        )

    def fin_to(other):
        return send(fin.at[other], out.at[me], last_send, out_recv, {"px": other})

    def over_px(body):
        def one_step(at, _):
            body(lax.rem(me + at, npx))
            return 0

        lax.fori_loop(1, npx, one_step, 0)

    @pl.when(x_first)
    def _():
        whole(lines, lines_come).wait()
        whole(fix_recv.at[my], fix_come).wait()
        for p in range(npx):
            fix_rows[2 * p : 2 * p + 2, :] = fix_recv[my, p, :, 0:rows]
        fix_cols[...] = jnp.transpose(fix_rows[...])
        for p in range(npx):
            mend(lines, p, 0, lambda end: fix_cols[:, 2 * p + end : 2 * p + end + 1])
            for end in range(2):
                mend_row(lines, p, (rows - 16) * end, end, 0, fix_recv[my, p, end : end + 1, rows : rows + cols])
        loads[4].wait()
        for step in order:
            other = mate(step)
            mine = ix[:, rows_of(other), :].reshape(npx * part, order_x)
            value = jnp.dot(mine, lines[...].reshape(order_x, cols), preferred_element_type=jnp.float32)
            mid[other] = narrow(value, (npx, part, cols))
            if step:
                mid_to_cross(other, my).start()
            else:
                pltpu.make_async_copy(mid.at[my], cross.at[:, :, strip(my)], cross_come).start()
        whole(mid.at[pl.ds(0, npy - 1)], mid_send).wait()
        loads[5].wait()
        whole(cross, cross_come).wait()
        for step in (0, *order[:-1]):
            other = mate(step)
            value = lax.dot_general(
                cross[...].reshape(npx * part, order_y),
                iy[strip(other), :],
                (((1,), (1,)), ((), ())),
                preferred_element_type=jnp.float32,
            )
            two[pl.ds(other * npx, npx)] = narrow(value, (npx, part, cols))
            if not step:
                over_px(lambda other_x: two_to(my, other_x, last_send).start())
                pltpu.make_async_copy(two.at[my * npx + me], out.at[me, rows_of(my), :], out_recv).start()
        pl.semaphore_wait(gate, 1)
        for step in range(npy - 1, 0, -1):
            other = mate(step)
            over_px(lambda other_x: two_to(other, other_x, last_send).start())
            two_to(other, me, last_send).start()

    @pl.when(jnp.logical_not(x_first))
    def _():
        def pass_level(at, _):
            whole(relay.at[at], relay_come.at[at]).wait()
            for step in range(1, npy):
                for core in range(2):
                    pass_on(at, core, mate(step))
            return 0

        lax.fori_loop(0, pairs - 1, pass_level, 0)
        outer = (my == 0) | (my == npy - 1)

        @pl.when(outer)
        def _():
            whole(fix_recv, fix_come).wait()

        @pl.when(jnp.logical_not(outer))
        def _():
            whole(fix_recv.at[:, :, :, pl.ds(0, rows)], fix_come).wait()

        for q in range(npy):
            for p in range(npx):
                at = 2 * (q * npx + p)
                fix_rows[at : at + 2, :] = fix_recv[q, p, :, 0:rows]
        fix_cols[...] = jnp.transpose(fix_rows[...])
        whole(cross, cross_come).wait()
        for q in range(npy):
            for p in range(npx):
                at = 2 * (q * npx + p)
                mend(cross, p, q * cols, lambda end: fix_cols[rows_of(my), at + end : at + end + 1])
        for end in range(2):
            @pl.when(my == (npy - 1) * end)
            def _():
                for q in range(npy):
                    for p in range(npx):
                        value = fix_recv[q, p, end : end + 1, rows : rows + cols]
                        mend_row(cross, p, (part - 16) * end, end, q * cols, value)

        loads[5].wait()
        for step in order:
            other = mate(step)
            value = lax.dot_general(
                cross[...].reshape(npx * part, order_y),
                iy[strip(other), :],
                (((1,), (1,)), ((), ())),
                preferred_element_type=jnp.float32,
            )
            mid[other] = narrow(value, (npx, part, cols))
        pltpu.make_async_copy(mid.at[my], lines.at[:, rows_of(my), :], lines_come).start()
        for step in range(npy - 1, 0, -1):
            mid_to_lines(mate(step), my).start()
        whole(mid.at[pl.ds(0, npy - 1)], mid_send).wait()
        pl.semaphore_signal(gate, inc=1, device_id={"px": twin}, device_id_type=pl.DeviceIdType.MESH)
        loads[4].wait()
        whole(lines, lines_come).wait()
        half = npx // pairs
        for at in range(pairs):
            first = half * lax.rem(me // half + 1 + at, pairs)
            value = jnp.dot(
                ix[pl.ds(first, half)].reshape(half * rows, order_x),
                lines[...].reshape(order_x, cols),
                preferred_element_type=jnp.float32,
            )
            fin[pl.ds(first, half)] = narrow(value, (half, rows, cols))
            for other in (first, first + 1):
                @pl.when(other != me)
                def _():
                    fin_to(other).start()

                @pl.when(other == me)
                def _():
                    pltpu.make_async_copy(fin.at[me], out.at[me], out_recv).start()

    whole(x_send, x_sent).wait()
    whole(y_send, y_sent).wait()

    whole(rhs.at[pl.ds(0, levels - 1)], rhs_send).wait()

    def fix_done(level, _):
        @pl.when((level != me) & (lax.rem(level, 2) == 0))
        def _():
            fix_to(level, my, fix_sent, rows + cols).wait_send()

        for plane in range(npy):
            @pl.when((lax.rem(level, 2) == 1) & ((level != me) | (plane != my)))
            def _():
                fix_to(level, plane, fix_sent, fix_lanes(plane)).wait_send()

        return 0

    lax.fori_loop(0, levels, fix_done, 0)

    @pl.when(x_first)
    def _():
        whole(two.at[pl.ds(0, npy * npx - 1)], last_send).wait()

    @pl.when(jnp.logical_not(x_first))
    def _():
        whole(rhs.at[me, pl.ds(0, rows - part)], own_send).wait()
        whole(relay, pass_send).wait()
        whole(fin.at[pl.ds(0, npx - 1)], last_send).wait()

    whole(out, out_recv).wait()


def fused(velocity, forcing, cross_x, cross_y, inv_x, inv_y):
    npx, npy = lax.axis_size("px"), lax.axis_size("py")
    levels, rows, cols = velocity.shape
    part = rows // npy
    shape, narrow = velocity.shape, jnp.bfloat16
    order_x, order_y = npx * rows, npy * cols
    vmem, dma = pltpu.VMEM, pltpu.SemaphoreType.DMA
    settled = pl.pallas_call(
        functools.partial(kernel, npx, npy),
        out_shape=jax.ShapeDtypeStruct(shape, narrow),
        in_specs=[pl.BlockSpec(memory_space=pl.ANY)] * 6,
        out_specs=pl.BlockSpec(memory_space=pl.ANY),
        scratch_shapes=[
            vmem(shape, jnp.float32),
            vmem(shape, narrow),
            vmem(shape, narrow),
            vmem(shape, narrow),
            vmem((npx, rows, order_x), narrow),
            vmem((order_y, order_y), narrow),
            vmem((2, levels, cols), jnp.float32),
            vmem((2, levels, cols), jnp.float32),
            vmem((2, levels, cols), jnp.float32),
            vmem((2, levels, rows), jnp.float32),
            vmem((2, levels, rows), jnp.float32),
            vmem((2, levels, rows), jnp.float32),
            vmem((levels, rows, cols), narrow),
            vmem((npx, rows, cols), narrow),
            vmem((npx // 2 - 1, npy - 1, 2, part, cols), narrow),
            vmem((npx, part, order_y), narrow),
            vmem((npy, npx, part, cols), narrow),
            vmem((npy * npx, part, cols), narrow),
            vmem((npx, rows, cols), narrow),
            vmem((levels, 2, rows + cols), jnp.float32),
            vmem((npy, npx, 2, rows + cols), jnp.float32),
            vmem((128, rows), jnp.float32),
            vmem((rows, 128), jnp.float32),
            dma((6,)),
            dma((npx // 2 - 1,)),
            *[dma] * 14,
            *[pltpu.SemaphoreType.REGULAR] * 2,
        ],
        compiler_params=pltpu.CompilerParams(collective_id=0, has_side_effects=True, vmem_limit_bytes=56_000_000),
        cost_estimate=pl.CostEstimate(flops=4 * order_x * order_y * rows, bytes_accessed=8 * 1024 * 1024, transcendentals=0),
    )(
        velocity,
        forcing,
        cross_x,
        cross_y,
        inv_x.reshape(npx, rows, order_x),
        inv_y.reshape(order_y, order_y),
    )
    return velocity + settled.astype(jnp.float32)


def step(velocity, forcing, cross_x, cross_y, inv_x, inv_y):
    npx, npy = lax.axis_size("px"), lax.axis_size("py")
    levels, rows, cols = velocity.shape
    aligned = rows % (32 * npy) == 0 and rows % 128 == 0 and cols % 128 == 0 and levels % 8 == 0
    paired = npx % 2 == 0 and npx > 2 and npy > 1 and 2 * npx * npy <= 128
    if aligned and paired and levels == npx and inv_x.shape[0] == 1:
        return fused(velocity, forcing, cross_x, cross_y, inv_x, inv_y)
    return shards(velocity, forcing, cross_x, cross_y, inv_x, inv_y)


def solution(mesh):
    return jax.shard_map(
        step,
        mesh=mesh,
        in_specs=(
            P(None, "px", "py"),
            P(None, "px", "py"),
            P(None, "px", "py"),
            P(None, "px", "py"),
            P("px", None, None),
            P("px", None, None),
        ),
        out_specs=P(None, "px", "py"),
        check_vma=False,
    )
```

```python
import functools

import jax
import jax.numpy as jnp
from jax import lax
from jax.experimental import pallas as pl
from jax.experimental.pallas import tpu as pltpu
from jax.sharding import PartitionSpec as P

time_step = 0.25


def with_halo(cells, sides, width):
    for axis, dim in sides:
        count = lax.axis_size(axis)
        head = lax.slice_in_dim(cells, 0, width, axis=dim)
        tail = lax.slice_in_dim(cells, cells.shape[dim] - width, cells.shape[dim], axis=dim)
        cells = jnp.concatenate(
            [
                lax.ppermute(tail, axis, [(i, (i + 1) % count) for i in range(count)]),
                cells,
                lax.ppermute(head, axis, [((i + 1) % count, i) for i in range(count)]),
            ],
            axis=dim,
        )
    return cells


def shards(velocity, forcing, cross_x, cross_y, inv_x, inv_y):
    padded = with_halo(velocity, (("px", 1), ("py", 2)), 1)
    x_plus = padded[:, 2:, 1:-1]
    x_minus = padded[:, :-2, 1:-1]
    y_plus = padded[:, 1:-1, 2:]
    y_minus = padded[:, 1:-1, :-2]
    z_padded = jnp.pad(velocity, ((1, 1), (0, 0), (0, 0)))
    laplace = (
        x_plus
        + x_minus
        + y_plus
        + y_minus
        - 4.0 * velocity
        + z_padded[2:]
        + z_padded[:-2]
        - 2.0 * velocity
    )
    slope_x = jnp.pad(0.5 * (x_plus - x_minus), ((1, 1), (0, 0), (0, 0)))
    slope_y = jnp.pad(0.5 * (y_plus - y_minus), ((1, 1), (0, 0), (0, 0)))
    mixed_x = 0.5 * (slope_x[2:] - slope_x[:-2])
    mixed_y = 0.5 * (slope_y[2:] - slope_y[:-2])
    total = (
        laplace
        + cross_x.astype(jnp.float32) * mixed_x
        + cross_y.astype(jnp.float32) * mixed_y
        + forcing.astype(jnp.float32)
    )
    rhs = (time_step * total).astype(jnp.bfloat16)
    section_one = jnp.einsum(
        "lab,lbk->lak",
        inv_x,
        lax.all_to_all(rhs, "px", split_axis=0, concat_axis=1, tiled=True),
        preferred_element_type=jnp.float32,
    ).astype(jnp.bfloat16)
    y_lines = lax.all_to_all(section_one, "py", split_axis=1, concat_axis=2, tiled=True)
    section_two = jnp.einsum("lxb,lab->lxa", y_lines, inv_y, preferred_element_type=jnp.float32)
    settled = lax.all_to_all(
        lax.all_to_all(section_two, "py", split_axis=2, concat_axis=1, tiled=True),
        "px",
        split_axis=1,
        concat_axis=0,
        tiled=True,
    )
    return velocity + settled


def send(src, dst, send_sem, recv_sem, target):
    return pltpu.make_async_remote_copy(
        src_ref=src,
        dst_ref=dst,
        send_sem=send_sem,
        recv_sem=recv_sem,
        device_id=target,
        device_id_type=pl.DeviceIdType.MESH,
    )


def kernel(
    npx,
    npy,
    vel_hbm,
    frc_hbm,
    cx_hbm,
    cy_hbm,
    ix_hbm,
    iy_hbm,
    out,
    vel,
    frc,
    cx,
    cy,
    ix,
    iy,
    x_send,
    x_recv,
    cx_ends,
    y_send,
    y_recv,
    cy_ends,
    rhs,
    lines,
    relay,
    cross,
    mid,
    two,
    fin,
    fix_send,
    fix_recv,
    row_recv,
    spread,
    delta,
    extra,
    load_sem,
    relay_come,
    x_sent,
    x_come,
    y_sent,
    y_come,
    rhs_send,
    own_send,
    fix_sent,
    fix_come,
    row_come,
    lines_come,
    cross_come,
    pass_send,
    mid_send,
    last_send,
    out_recv,
    ready,
    gate,
):
    me = lax.axis_index("px")
    my = lax.axis_index("py")
    levels, rows, cols = vel.shape
    part = rows // npy
    order_x, order_y = npx * rows, npy * cols
    x_first = lax.rem(me, 2) == 0
    pieces = [(vel_hbm, vel), (frc_hbm, frc), (cx_hbm, cx), (cy_hbm, cy), (ix_hbm, ix), (iy_hbm, iy)]
    loads = [pltpu.make_async_copy(a, b, load_sem.at[i]) for i, (a, b) in enumerate(pieces)]
    for load in loads:
        load.start()

    def whole(ref, sem):
        return pltpu.make_async_copy(ref, ref, sem)

    barrier = pltpu.get_barrier_semaphore()

    def greet(where):
        pl.semaphore_signal(barrier, inc=1, device_id=where, device_id_type=pl.DeviceIdType.MESH)

    twin = me + 1 - 2 * lax.rem(me, 2)
    for step in range(1, npy):
        other = lax.rem(my + step, npy)
        greet({"py": other})
        greet({"px": twin, "py": other})
    for step in range(1, npx):
        greet({"px": lax.rem(me + step, npx)})
    spread[...] = jnp.zeros_like(spread)
    delta[...] = jnp.zeros_like(delta)
    loads[0].wait()
    lane = lax.broadcasted_iota(jnp.int32, (rows, 128), 1)
    zero = jnp.zeros((rows, 128), jnp.float32)

    for level in range(levels):
        x_send[0, level : level + 1, :] = vel[level, 0:1, :]
        x_send[1, level : level + 1, :] = vel[level, rows - 1 : rows, :]
    first, last = zero, zero
    for level in range(levels):
        first = jnp.where(lane == level, vel[level, :, 0:1], first)
        last = jnp.where(lane == level, vel[level, :, cols - 1 : cols], last)
    y_send[0], y_send[1] = jnp.transpose(first)[:levels], jnp.transpose(last)[:levels]
    pl.semaphore_wait(barrier, npx - 1 + 2 * (npy - 1))

    up_x, down_x = lax.rem(me + 1, npx), lax.rem(me + npx - 1, npx)
    up_y, down_y = lax.rem(my + 1, npy), lax.rem(my + npy - 1, npy)
    halos_y = [
        send(y_send.at[1], y_recv.at[0], y_sent, y_come, {"py": up_y}),
        send(y_send.at[0], y_recv.at[1], y_sent, y_come, {"py": down_y}),
    ]
    halos_x = [
        send(x_send.at[1], x_recv.at[0], x_sent, x_come, {"px": up_x}),
        send(x_send.at[0], x_recv.at[1], x_sent, x_come, {"px": down_x}),
    ]
    for halo in halos_y + halos_x:
        halo.start()
    for step in range(2, npy - 1):
        pl.semaphore_signal(
            ready, inc=1, device_id={"py": lax.rem(my + step, npy)}, device_id_type=pl.DeviceIdType.MESH
        )
    for load in loads[1:4]:
        load.wait()

    def strip(at):
        return pl.ds(pl.multiple_of(at * cols, cols), cols)

    def rows_of(at):
        return pl.ds(pl.multiple_of(at * part, part), part)

    def inner(level):
        now = vel[level]
        above = jnp.where(level < levels - 1, 1.0, 0.0) * vel[jnp.minimum(level + 1, levels - 1)]
        below = jnp.where(level > 0, 1.0, 0.0) * vel[jnp.maximum(level - 1, 0)]
        rise = above - below
        total = pltpu.roll(now, 1, 0) + pltpu.roll(now, rows - 1, 0) + pltpu.roll(now, 1, 1) + pltpu.roll(now, cols - 1, 1)
        total += above + below - 6.0 * now + frc[level].astype(jnp.float32)
        total += cx[level].astype(jnp.float32) * (0.25 * (pltpu.roll(rise, rows - 1, 0) - pltpu.roll(rise, 1, 0)))
        total += cy[level].astype(jnp.float32) * (0.25 * (pltpu.roll(rise, cols - 1, 1) - pltpu.roll(rise, 1, 1)))
        rhs[level] = (time_step * total).astype(jnp.bfloat16)

    def to_cross(level, other):
        src, dst = rhs.at[level, rows_of(other), :], cross.at[me, :, strip(my)]

        def away(sem):
            return send(src, dst, sem, cross_come, {"px": level, "py": other})

        @pl.when(level != me)
        def _():
            away(rhs_send).start()

        @pl.when((level == me) & (other != my))
        def _():
            away(own_send).start()

        @pl.when((level == me) & (other == my))
        def _():
            pltpu.make_async_copy(src, dst, cross_come).start()

    def gap(source, target):
        return lax.rem(source - target + npy, npy) - 1

    def to_relay(at, level, other):
        send(
            rhs.at[level, rows_of(other), :],
            relay.at[at, gap(my, other), lax.rem(me, 2)],
            rhs_send,
            relay_come.at[at],
            {"px": 2 * (me // 2) + 1, "py": other},
        ).start()

    turn = jnp.where(my < npy // 2, 1, npy - 1)

    def mate(step):
        return lax.rem(my + step * turn, npy)

    def to_lines(level):
        @pl.when(level != me)
        def _():
            send(rhs.at[level], lines.at[me], rhs_send, lines_come, {"px": level}).start()

        @pl.when(level == me)
        def _():
            pltpu.make_async_copy(rhs.at[level], lines.at[me], lines_come).start()

    pairs = npx // 2

    def level_of(at, odd):
        return 2 * lax.rem(me // 2 + 1 + at, pairs) + odd

    here = level_of(pairs - 1, 1)

    def one_pair(at, _):
        odd = level_of(at, 1)
        inner(odd)
        for step in range(npy - 1, 0, -1):
            to_relay(at, odd, mate(step))
        even = level_of(at, 0)
        inner(even)
        to_lines(even)
        return 0

    def near_odd(at, _):
        to_cross(level_of(at, 1), my)
        return 0

    lax.fori_loop(0, pairs - 1, one_pair, 0)
    inner(here - 1)
    to_lines(here - 1)
    inner(here)
    def level_slope(face):
        at = lax.broadcasted_iota(jnp.int32, face.shape, 0)
        lower = jnp.where(at == 0, 0.0, pltpu.roll(face, 1, 0))
        upper = jnp.where(at == levels - 1, 0.0, pltpu.roll(face, levels - 1, 0))
        return 0.25 * (upper - lower)

    pick_row = lax.broadcasted_iota(jnp.int32, (16, cols), 0)
    pick_col = lax.broadcasted_iota(jnp.int32, (16, cols), 1)
    pick = ((pick_row == 0) & (pick_col == 0)) | ((pick_row == 1) & (pick_col == cols - 1))
    picked = lax.dot_general(
        pick.astype(jnp.bfloat16), cy[...].reshape(levels * rows, cols), (((1,), (1,)), ((), ())), preferred_element_type=jnp.float32
    )
    for end in range(2):
        for level in range(levels):
            cy_ends[end, level : level + 1, :] = picked[end : end + 1, level * rows : (level + 1) * rows]
    for level in range(levels):
        cx_ends[0, level : level + 1, :] = cx[level, 0:16, :].astype(jnp.float32)[0:1]
        cx_ends[1, level : level + 1, :] = cx[level, rows - 16 : rows, :].astype(jnp.float32)[15:16]

    def correct(end, came, gone, metric, lanes):
        face = came[end] - gone[1 - end]
        mixed = level_slope(face) if end else -level_slope(face)
        value = time_step * (face + metric[end] * mixed)
        for level in range(levels):
            fix_send[level, end : end + 1, lanes] = value[level : level + 1, :]

    def row_to(level):
        return send(fix_send.at[level, :, pl.ds(rows, cols)], row_recv.at[me], fix_sent, row_come, {"px": level})

    def give_row(at, _):
        level = level_of(at, 0)

        @pl.when(level != me)
        def _():
            row_to(level).start()

        @pl.when(level == me)
        def _():
            pltpu.make_async_copy(fix_send.at[level, :, pl.ds(rows, cols)], row_recv.at[me], row_come).start()

        return 0

    whole(x_recv, x_come).wait()
    for end in range(2):
        correct(end, x_recv, x_send, cx_ends, slice(rows, rows + cols))
    lax.fori_loop(0, pairs, give_row, 0)
    whole(y_recv, y_come).wait()
    for end in range(2):
        correct(end, y_recv, y_send, cy_ends, slice(0, rows))
    if npy > 3:
        pl.semaphore_wait(ready, npy - 3)

    def fix_to(level, other, sem, lanes):
        return send(
            fix_send.at[level, :, pl.ds(0, lanes)],
            fix_recv.at[my, me, :, pl.ds(0, lanes)],
            sem,
            fix_come,
            {"px": level, "py": other},
        )

    def fix_here(level, lanes):
        pltpu.make_async_copy(
            fix_send.at[level, :, pl.ds(0, lanes)], fix_recv.at[my, me, :, pl.ds(0, lanes)], fix_come
        ).start()

    def fix_lanes(other, odd):
        return rows + cols if odd and other in (0, npy - 1) else rows

    def give(at, odd):
        level = level_of(at, odd)
        for other in range(npy):
            mine = (level == me) & (other == my)

            @pl.when(jnp.logical_not(mine))
            def _():
                fix_to(level, other, fix_sent, fix_lanes(other, odd)).start()

            @pl.when(mine)
            def _():
                fix_here(level, fix_lanes(other, odd))

        return 0

    lax.fori_loop(0, pairs, lambda at, _: give(at, 0), 0)
    lax.fori_loop(0, pairs, lambda at, _: give(at, 1), 0)
    for step in range(npy - 1, -1, -1):
        to_cross(here, mate(step))
    lax.fori_loop(0, pairs - 1, near_odd, 0)

    order = [*range(1, npy), 0]
    def narrow(value, shape):
        return value.astype(jnp.bfloat16).reshape(shape)

    def prepare(matrix):
        for q in range(npy):
            for p in range(npx):
                spread[2 * q : 2 * q + 2, p * rows : (p + 1) * rows] = fix_recv[q, p, :, 0:rows]
        moved = lax.dot_general(
            spread[...].astype(jnp.bfloat16), matrix, (((1,), (1,)), ((), ())), preferred_element_type=jnp.float32
        )
        spare = jnp.zeros((128 - moved.shape[0], moved.shape[1]), jnp.float32)
        moved = jnp.transpose(jnp.concatenate([moved, spare], axis=0))
        spot = lax.broadcasted_iota(jnp.int32, moved.shape, 1)
        for q in range(npy):
            for end in range(2):
                tile = slice(q * cols + (cols - 128) * end, q * cols + (cols - 128) * end + 128)
                column = moved[:, 2 * q + end : 2 * q + end + 1]
                now = delta[:, tile].astype(jnp.float32)
                delta[:, tile] = (now + jnp.where(spot == 127 * end, column, 0.0)).astype(jnp.bfloat16)

    def across(ref, other):
        return lax.dot_general(
            ref, iy[strip(other), :], (((1,), (1,)), ((), ())), preferred_element_type=jnp.float32
        )

    def prepare_extra():
        loads[5].wait()

        def one(q, _):
            extra[q] = across(delta[...], q)
            return 0

        lax.fori_loop(0, npy, one, 0)

    def mend_row(ref, at, first, end, where_cols, value):
        spot = lax.broadcasted_iota(jnp.int32, (16, cols), 0) == 15 * end
        block = (*at, slice(first, first + 16), slice(where_cols, where_cols + cols))
        ref[block] = (ref[block].astype(jnp.float32) + jnp.where(spot, value, 0.0)).astype(jnp.bfloat16)

    def mid_to_cross(other, source):
        return send(mid.at[other], cross.at[:, :, strip(source)], mid_send, cross_come, {"py": other})

    def mid_to_lines(other, source):
        return send(mid.at[other], lines.at[:, rows_of(source), :], mid_send, lines_come, {"py": other})

    def pass_on(at, core, source):
        send(
            relay.at[at, gap(source, my), core],
            cross.at[2 * (me // 2) + core, :, strip(source)],
            pass_send,
            cross_come,
            {"px": level_of(at, 1)},
        ).start()

    def two_to(other_y, other_x, sem):
        return send(
            two.at[other_y * npx + other_x], out.at[me, rows_of(my), :], sem, out_recv, {"px": other_x, "py": other_y}
        )

    def fin_to(other):
        return send(fin.at[other], out.at[me], last_send, out_recv, {"px": other})

    def away_px(body):
        def one_step(at, _):
            body(lax.rem(2 * (me // 2) + at, npx))
            return 0

        lax.fori_loop(2, npx, one_step, 0)

    def over_px(body):
        def one_step(at, _):
            body(lax.rem(me + at, npx))
            return 0

        lax.fori_loop(1, npx, one_step, 0)

    @pl.when(x_first)
    def _():
        whole(lines, lines_come).wait()
        whole(row_recv, row_come).wait()
        for p in range(npx):
            for end in range(2):
                mend_row(lines, (p,), (rows - 16) * end, end, 0, row_recv[p, end : end + 1, :])
        loads[4].wait()
        for step in order:
            other = mate(step)
            mine = ix[:, rows_of(other), :].reshape(npx * part, order_x)
            value = jnp.dot(mine, lines[...].reshape(order_x, cols), preferred_element_type=jnp.float32)
            mid[other] = narrow(value, (npx, part, cols))
            if step:
                mid_to_cross(other, my).start()
            else:
                pltpu.make_async_copy(mid.at[my], cross.at[:, :, strip(my)], cross_come).start()
        whole(fix_recv.at[:, :, :, pl.ds(0, rows)], fix_come).wait()
        prepare(ix[:, rows_of(my), :].reshape(npx * part, order_x))
        prepare_extra()
        whole(mid.at[pl.ds(0, npy - 1)], mid_send).wait()
        whole(cross, cross_come).wait()
        for step in (0, *order[:-1]):
            other = mate(step)
            value = across(cross[...].reshape(npx * part, order_y), other) + extra[other]
            two[pl.ds(other * npx, npx)] = narrow(value, (npx, part, cols))
            if not step:
                over_px(lambda other_x: two_to(my, other_x, last_send).start())
                pltpu.make_async_copy(two.at[my * npx + me], out.at[me, rows_of(my), :], out_recv).start()
        pl.semaphore_wait(gate, 1)
        for step in range(npy - 1, 0, -1):
            other = mate(step)
            two_to(other, twin, last_send).start()
            two_to(other, me, last_send).start()
        for step in range(npy - 1, 0, -1):
            other = mate(step)
            away_px(lambda other_x: two_to(other, other_x, last_send).start())

    @pl.when(jnp.logical_not(x_first))
    def _():
        def pass_level(at, _):
            whole(relay.at[at], relay_come.at[at]).wait()
            for step in range(1, npy):
                for core in range(2):
                    pass_on(at, core, mate(step))
            return 0

        lax.fori_loop(0, pairs - 1, pass_level, 0)
        outer = (my == 0) | (my == npy - 1)

        @pl.when(outer)
        def _():
            whole(fix_recv, fix_come).wait()

        @pl.when(jnp.logical_not(outer))
        def _():
            whole(fix_recv.at[:, :, :, pl.ds(0, rows)], fix_come).wait()

        line = lax.broadcasted_iota(jnp.int32, (npx * part, order_x), 0)
        column = lax.broadcasted_iota(jnp.int32, (npx * part, order_x), 1)
        prepare((column == line // part * rows + my * part + lax.rem(line, part)).astype(jnp.bfloat16))
        for end in range(2):
            @pl.when(my == (npy - 1) * end)
            def _():
                for q in range(npy):
                    for p in range(npx):
                        value = fix_recv[q, p, end : end + 1, rows : rows + cols]
                        mend_row(delta, (), p * part + (part - 16) * end, end, q * cols, value)

        prepare_extra()
        whole(cross, cross_come).wait()
        for step in (*range(npy - 1, 0, -1), 0):
            other = mate(step)
            value = across(cross[...].reshape(npx * part, order_y), other) + extra[other]
            mid[other] = narrow(value, (npx, part, cols))
            if step:
                mid_to_lines(other, my).start()
        pltpu.make_async_copy(mid.at[my], lines.at[:, rows_of(my), :], lines_come).start()
        whole(mid.at[pl.ds(0, npy - 1)], mid_send).wait()
        pl.semaphore_signal(gate, inc=1, device_id={"px": twin}, device_id_type=pl.DeviceIdType.MESH)
        loads[4].wait()
        whole(lines, lines_come).wait()
        half = npx // pairs
        for at in range(pairs):
            first = half * lax.rem(me // half + 1 + at, pairs)
            value = jnp.dot(
                ix[pl.ds(first, half)].reshape(half * rows, order_x),
                lines[...].reshape(order_x, cols),
                preferred_element_type=jnp.float32,
            )
            fin[pl.ds(first, half)] = narrow(value, (half, rows, cols))
            for other in (first, first + 1):
                @pl.when(other != me)
                def _():
                    fin_to(other).start()

                @pl.when(other == me)
                def _():
                    pltpu.make_async_copy(fin.at[me], out.at[me], out_recv).start()

    whole(x_send, x_sent).wait()
    whole(y_send, y_sent).wait()

    whole(rhs.at[pl.ds(0, levels - 1)], rhs_send).wait()

    def fix_done(level, _):
        odd = lax.rem(level, 2)

        @pl.when((level != me) & (odd == 0))
        def _():
            row_to(level).wait_send()

        for kind in range(2):
            for plane in range(npy):
                @pl.when((odd == kind) & ((level != me) | (plane != my)))
                def _():
                    fix_to(level, plane, fix_sent, fix_lanes(plane, kind)).wait_send()

        return 0

    lax.fori_loop(0, levels, fix_done, 0)

    @pl.when(x_first)
    def _():
        whole(two.at[pl.ds(0, npy * npx - 1)], last_send).wait()

    @pl.when(jnp.logical_not(x_first))
    def _():
        whole(rhs.at[me, pl.ds(0, rows - part)], own_send).wait()
        whole(relay, pass_send).wait()
        whole(fin.at[pl.ds(0, npx - 1)], last_send).wait()

    whole(out, out_recv).wait()


def fused(velocity, forcing, cross_x, cross_y, inv_x, inv_y):
    npx, npy = lax.axis_size("px"), lax.axis_size("py")
    levels, rows, cols = velocity.shape
    part = rows // npy
    shape, narrow = velocity.shape, jnp.bfloat16
    order_x, order_y = npx * rows, npy * cols
    vmem, dma = pltpu.VMEM, pltpu.SemaphoreType.DMA
    settled = pl.pallas_call(
        functools.partial(kernel, npx, npy),
        out_shape=jax.ShapeDtypeStruct(shape, narrow),
        in_specs=[pl.BlockSpec(memory_space=pl.ANY)] * 6,
        out_specs=pl.BlockSpec(memory_space=pl.ANY),
        scratch_shapes=[
            vmem(shape, jnp.float32),
            vmem(shape, narrow),
            vmem(shape, narrow),
            vmem(shape, narrow),
            vmem((npx, rows, order_x), narrow),
            vmem((order_y, order_y), narrow),
            vmem((2, levels, cols), jnp.float32),
            vmem((2, levels, cols), jnp.float32),
            vmem((2, levels, cols), jnp.float32),
            vmem((2, levels, rows), jnp.float32),
            vmem((2, levels, rows), jnp.float32),
            vmem((2, levels, rows), jnp.float32),
            vmem((levels, rows, cols), narrow),
            vmem((npx, rows, cols), narrow),
            vmem((npx // 2 - 1, npy - 1, 2, part, cols), narrow),
            vmem((npx, part, order_y), narrow),
            vmem((npy, npx, part, cols), narrow),
            vmem((npy * npx, part, cols), narrow),
            vmem((npx, rows, cols), narrow),
            vmem((levels, 2, rows + cols), jnp.float32),
            vmem((npy, npx, 2, rows + cols), jnp.float32),
            vmem((npx, 2, cols), jnp.float32),
            vmem((-(-2 * npy // 16) * 16, order_x), jnp.float32),
            vmem((npx * part, order_y), narrow),
            vmem((npy, npx * part, cols), jnp.float32),
            dma((6,)),
            dma((npx // 2 - 1,)),
            *[dma] * 15,
            *[pltpu.SemaphoreType.REGULAR] * 2,
        ],
        compiler_params=pltpu.CompilerParams(collective_id=0, has_side_effects=True, vmem_limit_bytes=56_000_000),
        cost_estimate=pl.CostEstimate(flops=4 * order_x * order_y * rows, bytes_accessed=8 * 1024 * 1024, transcendentals=0),
    )(
        velocity,
        forcing,
        cross_x,
        cross_y,
        inv_x.reshape(npx, rows, order_x),
        inv_y.reshape(order_y, order_y),
    )
    return velocity + settled.astype(jnp.float32)


def step(velocity, forcing, cross_x, cross_y, inv_x, inv_y):
    npx, npy = lax.axis_size("px"), lax.axis_size("py")
    levels, rows, cols = velocity.shape
    aligned = rows % (32 * npy) == 0 and rows % 128 == 0 and cols % 128 == 0 and levels % 8 == 0
    paired = npx % 2 == 0 and npx > 2 and npy > 1 and 2 * npy <= 128
    if aligned and paired and levels == npx and inv_x.shape[0] == 1:
        return fused(velocity, forcing, cross_x, cross_y, inv_x, inv_y)
    return shards(velocity, forcing, cross_x, cross_y, inv_x, inv_y)


def solution(mesh):
    return jax.shard_map(
        step,
        mesh=mesh,
        in_specs=(
            P(None, "px", "py"),
            P(None, "px", "py"),
            P(None, "px", "py"),
            P(None, "px", "py"),
            P("px", None, None),
            P("px", None, None),
        ),
        out_specs=P(None, "px", "py"),
        check_vma=False,
    )
```

```python
import functools

import jax
import jax.numpy as jnp
from jax import lax
from jax.experimental import pallas as pl
from jax.experimental.pallas import tpu as pltpu
from jax.sharding import PartitionSpec as P

time_step = 0.25


def with_halo(cells, sides, width):
    for axis, dim in sides:
        count = lax.axis_size(axis)
        head = lax.slice_in_dim(cells, 0, width, axis=dim)
        tail = lax.slice_in_dim(cells, cells.shape[dim] - width, cells.shape[dim], axis=dim)
        cells = jnp.concatenate(
            [
                lax.ppermute(tail, axis, [(i, (i + 1) % count) for i in range(count)]),
                cells,
                lax.ppermute(head, axis, [((i + 1) % count, i) for i in range(count)]),
            ],
            axis=dim,
        )
    return cells


def shards(velocity, forcing, cross_x, cross_y, inv_x, inv_y):
    padded = with_halo(velocity, (("px", 1), ("py", 2)), 1)
    x_plus = padded[:, 2:, 1:-1]
    x_minus = padded[:, :-2, 1:-1]
    y_plus = padded[:, 1:-1, 2:]
    y_minus = padded[:, 1:-1, :-2]
    z_padded = jnp.pad(velocity, ((1, 1), (0, 0), (0, 0)))
    laplace = (
        x_plus
        + x_minus
        + y_plus
        + y_minus
        - 4.0 * velocity
        + z_padded[2:]
        + z_padded[:-2]
        - 2.0 * velocity
    )
    slope_x = jnp.pad(0.5 * (x_plus - x_minus), ((1, 1), (0, 0), (0, 0)))
    slope_y = jnp.pad(0.5 * (y_plus - y_minus), ((1, 1), (0, 0), (0, 0)))
    mixed_x = 0.5 * (slope_x[2:] - slope_x[:-2])
    mixed_y = 0.5 * (slope_y[2:] - slope_y[:-2])
    total = (
        laplace
        + cross_x.astype(jnp.float32) * mixed_x
        + cross_y.astype(jnp.float32) * mixed_y
        + forcing.astype(jnp.float32)
    )
    rhs = (time_step * total).astype(jnp.bfloat16)
    section_one = jnp.einsum(
        "lab,lbk->lak",
        inv_x,
        lax.all_to_all(rhs, "px", split_axis=0, concat_axis=1, tiled=True),
        preferred_element_type=jnp.float32,
    ).astype(jnp.bfloat16)
    y_lines = lax.all_to_all(section_one, "py", split_axis=1, concat_axis=2, tiled=True)
    section_two = jnp.einsum("lxb,lab->lxa", y_lines, inv_y, preferred_element_type=jnp.float32)
    settled = lax.all_to_all(
        lax.all_to_all(section_two, "py", split_axis=2, concat_axis=1, tiled=True),
        "px",
        split_axis=1,
        concat_axis=0,
        tiled=True,
    )
    return velocity + settled


def send(src, dst, send_sem, recv_sem, target):
    return pltpu.make_async_remote_copy(
        src_ref=src,
        dst_ref=dst,
        send_sem=send_sem,
        recv_sem=recv_sem,
        device_id=target,
        device_id_type=pl.DeviceIdType.MESH,
    )


def kernel(
    npx,
    npy,
    vel_hbm,
    frc_hbm,
    cx_hbm,
    cy_hbm,
    ix_hbm,
    iy_hbm,
    out,
    vel,
    frc,
    cx,
    cy,
    ix,
    iy,
    x_send,
    x_recv,
    cx_ends,
    y_send,
    y_recv,
    cy_ends,
    rhs,
    lines,
    relay,
    cross,
    mid,
    two,
    fin,
    fix_send,
    fix_recv,
    row_recv,
    spread,
    delta,
    extra,
    load_sem,
    relay_come,
    x_sent,
    x_come,
    y_sent,
    y_come,
    rhs_send,
    own_send,
    fix_sent,
    fix_come,
    row_come,
    lines_come,
    cross_come,
    pass_send,
    mid_send,
    last_send,
    out_recv,
    ready,
    gate,
):
    me = lax.axis_index("px")
    my = lax.axis_index("py")
    levels, rows, cols = vel.shape
    part = rows // npy
    order_x, order_y = npx * rows, npy * cols
    x_first = lax.rem(me, 2) == 0
    pieces = [(vel_hbm, vel), (frc_hbm, frc), (cx_hbm, cx), (cy_hbm, cy), (ix_hbm, ix), (iy_hbm, iy)]
    loads = [pltpu.make_async_copy(a, b, load_sem.at[i]) for i, (a, b) in enumerate(pieces)]
    for load in loads:
        load.start()

    def whole(ref, sem):
        return pltpu.make_async_copy(ref, ref, sem)

    barrier = pltpu.get_barrier_semaphore()

    def greet(where):
        pl.semaphore_signal(barrier, inc=1, device_id=where, device_id_type=pl.DeviceIdType.MESH)

    twin = me + 1 - 2 * lax.rem(me, 2)
    for step in range(1, npy):
        other = lax.rem(my + step, npy)
        greet({"py": other})
        greet({"px": twin, "py": other})
    for step in range(1, npx):
        greet({"px": lax.rem(me + step, npx)})
    spread[...] = jnp.zeros_like(spread)
    delta[...] = jnp.zeros_like(delta)
    loads[0].wait()
    lane = lax.broadcasted_iota(jnp.int32, (rows, 128), 1)
    zero = jnp.zeros((rows, 128), jnp.float32)

    for level in range(levels):
        x_send[0, level : level + 1, :] = vel[level, 0:1, :]
        x_send[1, level : level + 1, :] = vel[level, rows - 1 : rows, :]
    first, last = zero, zero
    for level in range(levels):
        first = jnp.where(lane == level, vel[level, :, 0:1], first)
        last = jnp.where(lane == level, vel[level, :, cols - 1 : cols], last)
    y_send[0], y_send[1] = jnp.transpose(first)[:levels], jnp.transpose(last)[:levels]
    pl.semaphore_wait(barrier, npx - 1 + 2 * (npy - 1))

    up_x, down_x = lax.rem(me + 1, npx), lax.rem(me + npx - 1, npx)
    up_y, down_y = lax.rem(my + 1, npy), lax.rem(my + npy - 1, npy)
    halos_y = [
        send(y_send.at[1], y_recv.at[0], y_sent, y_come, {"py": up_y}),
        send(y_send.at[0], y_recv.at[1], y_sent, y_come, {"py": down_y}),
    ]
    halos_x = [
        send(x_send.at[1], x_recv.at[0], x_sent, x_come, {"px": up_x}),
        send(x_send.at[0], x_recv.at[1], x_sent, x_come, {"px": down_x}),
    ]
    for halo in halos_y + halos_x:
        halo.start()
    for step in range(2, npy - 1):
        pl.semaphore_signal(
            ready, inc=1, device_id={"py": lax.rem(my + step, npy)}, device_id_type=pl.DeviceIdType.MESH
        )
    for load in loads[1:4]:
        load.wait()

    def strip(at):
        return pl.ds(pl.multiple_of(at * cols, cols), cols)

    def rows_of(at):
        return pl.ds(pl.multiple_of(at * part, part), part)

    def inner(level):
        now = vel[level]
        above = jnp.where(level < levels - 1, 1.0, 0.0) * vel[jnp.minimum(level + 1, levels - 1)]
        below = jnp.where(level > 0, 1.0, 0.0) * vel[jnp.maximum(level - 1, 0)]
        rise = above - below
        total = pltpu.roll(now, 1, 0) + pltpu.roll(now, rows - 1, 0) + pltpu.roll(now, 1, 1) + pltpu.roll(now, cols - 1, 1)
        total += above + below - 6.0 * now + frc[level].astype(jnp.float32)
        total += cx[level].astype(jnp.float32) * (0.25 * (pltpu.roll(rise, rows - 1, 0) - pltpu.roll(rise, 1, 0)))
        total += cy[level].astype(jnp.float32) * (0.25 * (pltpu.roll(rise, cols - 1, 1) - pltpu.roll(rise, 1, 1)))
        rhs[level] = (time_step * total).astype(jnp.bfloat16)

    def to_cross(level, other):
        src, dst = rhs.at[level, rows_of(other), :], cross.at[me, :, strip(my)]

        def away(sem):
            return send(src, dst, sem, cross_come, {"px": level, "py": other})

        @pl.when(level != me)
        def _():
            away(rhs_send).start()

        @pl.when((level == me) & (other != my))
        def _():
            away(own_send).start()

        @pl.when((level == me) & (other == my))
        def _():
            pltpu.make_async_copy(src, dst, cross_come).start()

    def gap(source, target):
        return lax.rem(source - target + npy, npy) - 1

    def to_relay(at, level, other):
        send(
            rhs.at[level, rows_of(other), :],
            relay.at[at, gap(my, other), lax.rem(me, 2)],
            rhs_send,
            relay_come.at[at],
            {"px": 2 * (me // 2) + 1, "py": other},
        ).start()

    turn = jnp.where(my < npy // 2, 1, npy - 1)

    def mate(step):
        return lax.rem(my + step * turn, npy)

    outermost = (my == 0) | (my == npy - 1)
    ahead = [*range(1, npy)]
    swapped = [*ahead[1::-1], *ahead[2:]]

    def peers(inner):
        return [mate(jnp.where(outermost, *steps)) for steps in zip(ahead, inner)]

    def to_lines(level):
        @pl.when(level != me)
        def _():
            send(rhs.at[level], lines.at[me], rhs_send, lines_come, {"px": level}).start()

        @pl.when(level == me)
        def _():
            pltpu.make_async_copy(rhs.at[level], lines.at[me], lines_come).start()

    pairs = npx // 2

    def level_of(at, odd):
        return 2 * lax.rem(me // 2 + 1 + at, pairs) + odd

    here = level_of(pairs - 1, 1)

    def one_pair(at, _):
        odd = level_of(at, 1)
        inner(odd)
        for step in range(npy - 1, 0, -1):
            to_relay(at, odd, mate(step))
        even = level_of(at, 0)
        inner(even)
        to_lines(even)
        return 0

    def near_odd(at, _):
        to_cross(level_of(at, 1), my)
        return 0

    lax.fori_loop(0, pairs - 1, one_pair, 0)
    inner(here - 1)
    to_lines(here - 1)
    inner(here)
    def level_slope(face):
        at = lax.broadcasted_iota(jnp.int32, face.shape, 0)
        lower = jnp.where(at == 0, 0.0, pltpu.roll(face, 1, 0))
        upper = jnp.where(at == levels - 1, 0.0, pltpu.roll(face, levels - 1, 0))
        return 0.25 * (upper - lower)

    pick_row = lax.broadcasted_iota(jnp.int32, (16, cols), 0)
    pick_col = lax.broadcasted_iota(jnp.int32, (16, cols), 1)
    pick = ((pick_row == 0) & (pick_col == 0)) | ((pick_row == 1) & (pick_col == cols - 1))
    picked = lax.dot_general(
        pick.astype(jnp.bfloat16), cy[...].reshape(levels * rows, cols), (((1,), (1,)), ((), ())), preferred_element_type=jnp.float32
    )
    for end in range(2):
        for level in range(levels):
            cy_ends[end, level : level + 1, :] = picked[end : end + 1, level * rows : (level + 1) * rows]
    for level in range(levels):
        cx_ends[0, level : level + 1, :] = cx[level, 0:16, :].astype(jnp.float32)[0:1]
        cx_ends[1, level : level + 1, :] = cx[level, rows - 16 : rows, :].astype(jnp.float32)[15:16]

    def correct(end, came, gone, metric, lanes):
        face = came[end] - gone[1 - end]
        mixed = level_slope(face) if end else -level_slope(face)
        value = time_step * (face + metric[end] * mixed)
        for level in range(levels):
            fix_send[level, end : end + 1, lanes] = value[level : level + 1, :]

    def row_to(level):
        return send(fix_send.at[level, :, pl.ds(rows, cols)], row_recv.at[me], fix_sent, row_come, {"px": level})

    def give_row(at, _):
        level = level_of(at, 0)

        @pl.when(level != me)
        def _():
            row_to(level).start()

        @pl.when(level == me)
        def _():
            pltpu.make_async_copy(fix_send.at[level, :, pl.ds(rows, cols)], row_recv.at[me], row_come).start()

        return 0

    whole(x_recv, x_come).wait()
    for end in range(2):
        correct(end, x_recv, x_send, cx_ends, slice(rows, rows + cols))
    lax.fori_loop(0, pairs, give_row, 0)
    whole(y_recv, y_come).wait()
    for end in range(2):
        correct(end, y_recv, y_send, cy_ends, slice(0, rows))
    if npy > 3:
        pl.semaphore_wait(ready, npy - 3)

    def fix_to(level, other, sem, lanes):
        return send(
            fix_send.at[level, :, pl.ds(0, lanes)],
            fix_recv.at[my, me, :, pl.ds(0, lanes)],
            sem,
            fix_come,
            {"px": level, "py": other},
        )

    def fix_here(level, lanes):
        pltpu.make_async_copy(
            fix_send.at[level, :, pl.ds(0, lanes)], fix_recv.at[my, me, :, pl.ds(0, lanes)], fix_come
        ).start()

    def fix_lanes(other, odd):
        return rows + cols if odd and other in (0, npy - 1) else rows

    def give(at, odd):
        level = level_of(at, odd)
        for other in range(npy):
            mine = (level == me) & (other == my)

            @pl.when(jnp.logical_not(mine))
            def _():
                fix_to(level, other, fix_sent, fix_lanes(other, odd)).start()

            @pl.when(mine)
            def _():
                fix_here(level, fix_lanes(other, odd))

        return 0

    lax.fori_loop(0, pairs, lambda at, _: give(at, 0), 0)
    lax.fori_loop(0, pairs, lambda at, _: give(at, 1), 0)
    for step in range(npy - 1, -1, -1):
        to_cross(here, mate(step))
    lax.fori_loop(0, pairs - 1, near_odd, 0)

    order = [*range(1, npy), 0]
    def narrow(value, shape):
        return value.astype(jnp.bfloat16).reshape(shape)

    def prepare(matrix):
        for q in range(npy):
            for p in range(npx):
                spread[2 * q : 2 * q + 2, p * rows : (p + 1) * rows] = fix_recv[q, p, :, 0:rows]
        moved = lax.dot_general(
            spread[...].astype(jnp.bfloat16), matrix, (((1,), (1,)), ((), ())), preferred_element_type=jnp.float32
        )
        spare = jnp.zeros((128 - moved.shape[0], moved.shape[1]), jnp.float32)
        moved = jnp.transpose(jnp.concatenate([moved, spare], axis=0))
        spot = lax.broadcasted_iota(jnp.int32, moved.shape, 1)
        for q in range(npy):
            for end in range(2):
                tile = slice(q * cols + (cols - 128) * end, q * cols + (cols - 128) * end + 128)
                column = moved[:, 2 * q + end : 2 * q + end + 1]
                now = delta[:, tile].astype(jnp.float32)
                delta[:, tile] = (now + jnp.where(spot == 127 * end, column, 0.0)).astype(jnp.bfloat16)

    def across(ref, other):
        return lax.dot_general(
            ref, iy[strip(other), :], (((1,), (1,)), ((), ())), preferred_element_type=jnp.float32
        )

    def prepare_extra():
        loads[5].wait()

        def one(q, _):
            extra[q] = across(delta[...], q)
            return 0

        lax.fori_loop(0, npy, one, 0)

    def mend_row(ref, at, first, end, where_cols, value):
        spot = lax.broadcasted_iota(jnp.int32, (16, cols), 0) == 15 * end
        block = (*at, slice(first, first + 16), slice(where_cols, where_cols + cols))
        ref[block] = (ref[block].astype(jnp.float32) + jnp.where(spot, value, 0.0)).astype(jnp.bfloat16)

    def mid_to_cross(other, source):
        return send(mid.at[other], cross.at[:, :, strip(source)], mid_send, cross_come, {"py": other})

    def mid_to_lines(other, source):
        return send(mid.at[other], lines.at[:, rows_of(source), :], mid_send, lines_come, {"py": other})

    def pass_on(at, core, source):
        send(
            relay.at[at, gap(source, my), core],
            cross.at[2 * (me // 2) + core, :, strip(source)],
            pass_send,
            cross_come,
            {"px": level_of(at, 1)},
        ).start()

    def two_to(other_y, other_x, sem):
        return send(
            two.at[other_y * npx + other_x], out.at[me, rows_of(my), :], sem, out_recv, {"px": other_x, "py": other_y}
        )

    def fin_to(other):
        return send(fin.at[other], out.at[me], last_send, out_recv, {"px": other})

    def away_px(body):
        def one_step(at, _):
            body(lax.rem(2 * (me // 2) + at, npx))
            return 0

        lax.fori_loop(2, npx, one_step, 0)

    def over_px(body):
        def one_step(at, _):
            body(lax.rem(me + at, npx))
            return 0

        lax.fori_loop(1, npx, one_step, 0)

    @pl.when(x_first)
    def _():
        whole(lines, lines_come).wait()
        whole(row_recv, row_come).wait()
        for p in range(npx):
            for end in range(2):
                mend_row(lines, (p,), (rows - 16) * end, end, 0, row_recv[p, end : end + 1, :])
        loads[4].wait()
        for other in (*peers(swapped), None):
            step, other = other is not None, my if other is None else other
            mine = ix[:, rows_of(other), :].reshape(npx * part, order_x)
            value = jnp.dot(mine, lines[...].reshape(order_x, cols), preferred_element_type=jnp.float32)
            mid[other] = narrow(value, (npx, part, cols))
            if step:
                mid_to_cross(other, my).start()
            else:
                pltpu.make_async_copy(mid.at[my], cross.at[:, :, strip(my)], cross_come).start()
        whole(fix_recv.at[:, :, :, pl.ds(0, rows)], fix_come).wait()
        prepare(ix[:, rows_of(my), :].reshape(npx * part, order_x))
        prepare_extra()
        whole(mid.at[pl.ds(0, npy - 1)], mid_send).wait()
        whole(cross, cross_come).wait()
        for step in (0, *order[:-1]):
            other = mate(step)
            value = across(cross[...].reshape(npx * part, order_y), other) + extra[other]
            two[pl.ds(other * npx, npx)] = narrow(value, (npx, part, cols))
            if not step:
                over_px(lambda other_x: two_to(my, other_x, last_send).start())
                pltpu.make_async_copy(two.at[my * npx + me], out.at[me, rows_of(my), :], out_recv).start()
        pl.semaphore_wait(gate, 1)
        for other in peers(ahead[::-1]):
            two_to(other, twin, last_send).start()
            two_to(other, me, last_send).start()
        for other in peers(ahead[::-1]):
            away_px(lambda other_x: two_to(other, other_x, last_send).start())

    @pl.when(jnp.logical_not(x_first))
    def _():
        def pass_level(at, _):
            whole(relay.at[at], relay_come.at[at]).wait()
            for step in range(1, npy):
                for core in range(2):
                    pass_on(at, core, mate(step))
            return 0

        lax.fori_loop(0, pairs - 1, pass_level, 0)
        outer = (my == 0) | (my == npy - 1)

        @pl.when(outer)
        def _():
            whole(fix_recv, fix_come).wait()

        @pl.when(jnp.logical_not(outer))
        def _():
            whole(fix_recv.at[:, :, :, pl.ds(0, rows)], fix_come).wait()

        line = lax.broadcasted_iota(jnp.int32, (npx * part, order_x), 0)
        column = lax.broadcasted_iota(jnp.int32, (npx * part, order_x), 1)
        prepare((column == line // part * rows + my * part + lax.rem(line, part)).astype(jnp.bfloat16))
        for end in range(2):
            @pl.when(my == (npy - 1) * end)
            def _():
                for q in range(npy):
                    for p in range(npx):
                        value = fix_recv[q, p, end : end + 1, rows : rows + cols]
                        mend_row(delta, (), p * part + (part - 16) * end, end, q * cols, value)

        prepare_extra()
        whole(cross, cross_come).wait()
        for other in (*peers(swapped), None):
            step, other = other is not None, my if other is None else other
            value = across(cross[...].reshape(npx * part, order_y), other) + extra[other]
            mid[other] = narrow(value, (npx, part, cols))
            if step:
                mid_to_lines(other, my).start()
        pltpu.make_async_copy(mid.at[my], lines.at[:, rows_of(my), :], lines_come).start()
        whole(mid.at[pl.ds(0, npy - 1)], mid_send).wait()
        pl.semaphore_signal(gate, inc=1, device_id={"px": twin}, device_id_type=pl.DeviceIdType.MESH)
        loads[4].wait()
        whole(lines, lines_come).wait()
        half = npx // pairs
        for at in range(pairs):
            first = half * lax.rem(me // half + 1 + at, pairs)
            value = jnp.dot(
                ix[pl.ds(first, half)].reshape(half * rows, order_x),
                lines[...].reshape(order_x, cols),
                preferred_element_type=jnp.float32,
            )
            fin[pl.ds(first, half)] = narrow(value, (half, rows, cols))
            for other in (first, first + 1):
                @pl.when(other != me)
                def _():
                    fin_to(other).start()

                @pl.when(other == me)
                def _():
                    pltpu.make_async_copy(fin.at[me], out.at[me], out_recv).start()

    whole(x_send, x_sent).wait()
    whole(y_send, y_sent).wait()

    whole(rhs.at[pl.ds(0, levels - 1)], rhs_send).wait()

    def fix_done(level, _):
        odd = lax.rem(level, 2)

        @pl.when((level != me) & (odd == 0))
        def _():
            row_to(level).wait_send()

        for kind in range(2):
            for plane in range(npy):
                @pl.when((odd == kind) & ((level != me) | (plane != my)))
                def _():
                    fix_to(level, plane, fix_sent, fix_lanes(plane, kind)).wait_send()

        return 0

    lax.fori_loop(0, levels, fix_done, 0)

    @pl.when(x_first)
    def _():
        whole(two.at[pl.ds(0, npy * npx - 1)], last_send).wait()

    @pl.when(jnp.logical_not(x_first))
    def _():
        whole(rhs.at[me, pl.ds(0, rows - part)], own_send).wait()
        whole(relay, pass_send).wait()
        whole(fin.at[pl.ds(0, npx - 1)], last_send).wait()

    whole(out, out_recv).wait()


def fused(velocity, forcing, cross_x, cross_y, inv_x, inv_y):
    npx, npy = lax.axis_size("px"), lax.axis_size("py")
    levels, rows, cols = velocity.shape
    part = rows // npy
    shape, narrow = velocity.shape, jnp.bfloat16
    order_x, order_y = npx * rows, npy * cols
    vmem, dma = pltpu.VMEM, pltpu.SemaphoreType.DMA
    settled = pl.pallas_call(
        functools.partial(kernel, npx, npy),
        out_shape=jax.ShapeDtypeStruct(shape, narrow),
        in_specs=[pl.BlockSpec(memory_space=pl.ANY)] * 6,
        out_specs=pl.BlockSpec(memory_space=pl.ANY),
        scratch_shapes=[
            vmem(shape, jnp.float32),
            vmem(shape, narrow),
            vmem(shape, narrow),
            vmem(shape, narrow),
            vmem((npx, rows, order_x), narrow),
            vmem((order_y, order_y), narrow),
            vmem((2, levels, cols), jnp.float32),
            vmem((2, levels, cols), jnp.float32),
            vmem((2, levels, cols), jnp.float32),
            vmem((2, levels, rows), jnp.float32),
            vmem((2, levels, rows), jnp.float32),
            vmem((2, levels, rows), jnp.float32),
            vmem((levels, rows, cols), narrow),
            vmem((npx, rows, cols), narrow),
            vmem((npx // 2 - 1, npy - 1, 2, part, cols), narrow),
            vmem((npx, part, order_y), narrow),
            vmem((npy, npx, part, cols), narrow),
            vmem((npy * npx, part, cols), narrow),
            vmem((npx, rows, cols), narrow),
            vmem((levels, 2, rows + cols), jnp.float32),
            vmem((npy, npx, 2, rows + cols), jnp.float32),
            vmem((npx, 2, cols), jnp.float32),
            vmem((-(-2 * npy // 16) * 16, order_x), jnp.float32),
            vmem((npx * part, order_y), narrow),
            vmem((npy, npx * part, cols), jnp.float32),
            dma((6,)),
            dma((npx // 2 - 1,)),
            *[dma] * 15,
            *[pltpu.SemaphoreType.REGULAR] * 2,
        ],
        compiler_params=pltpu.CompilerParams(collective_id=0, has_side_effects=True, vmem_limit_bytes=56_000_000),
        cost_estimate=pl.CostEstimate(flops=4 * order_x * order_y * rows, bytes_accessed=8 * 1024 * 1024, transcendentals=0),
    )(
        velocity,
        forcing,
        cross_x,
        cross_y,
        inv_x.reshape(npx, rows, order_x),
        inv_y.reshape(order_y, order_y),
    )
    return velocity + settled.astype(jnp.float32)


def step(velocity, forcing, cross_x, cross_y, inv_x, inv_y):
    npx, npy = lax.axis_size("px"), lax.axis_size("py")
    levels, rows, cols = velocity.shape
    aligned = rows % (32 * npy) == 0 and rows % 128 == 0 and cols % 128 == 0 and levels % 8 == 0
    paired = npx % 2 == 0 and npx > 2 and npy > 1 and 2 * npy <= 128
    if aligned and paired and levels == npx and inv_x.shape[0] == 1:
        return fused(velocity, forcing, cross_x, cross_y, inv_x, inv_y)
    return shards(velocity, forcing, cross_x, cross_y, inv_x, inv_y)


def solution(mesh):
    return jax.shard_map(
        step,
        mesh=mesh,
        in_specs=(
            P(None, "px", "py"),
            P(None, "px", "py"),
            P(None, "px", "py"),
            P(None, "px", "py"),
            P("px", None, None),
            P("px", None, None),
        ),
        out_specs=P(None, "px", "py"),
        check_vma=False,
    )
```

```python
import functools

import jax
import jax.numpy as jnp
from jax import lax
from jax.experimental import pallas as pl
from jax.experimental.pallas import tpu as pltpu
from jax.sharding import PartitionSpec as P

time_step = 0.25


def with_halo(cells, sides, width):
    for axis, dim in sides:
        count = lax.axis_size(axis)
        head = lax.slice_in_dim(cells, 0, width, axis=dim)
        tail = lax.slice_in_dim(cells, cells.shape[dim] - width, cells.shape[dim], axis=dim)
        cells = jnp.concatenate(
            [
                lax.ppermute(tail, axis, [(i, (i + 1) % count) for i in range(count)]),
                cells,
                lax.ppermute(head, axis, [((i + 1) % count, i) for i in range(count)]),
            ],
            axis=dim,
        )
    return cells


def shards(velocity, forcing, cross_x, cross_y, inv_x, inv_y):
    padded = with_halo(velocity, (("px", 1), ("py", 2)), 1)
    x_plus = padded[:, 2:, 1:-1]
    x_minus = padded[:, :-2, 1:-1]
    y_plus = padded[:, 1:-1, 2:]
    y_minus = padded[:, 1:-1, :-2]
    z_padded = jnp.pad(velocity, ((1, 1), (0, 0), (0, 0)))
    laplace = (
        x_plus
        + x_minus
        + y_plus
        + y_minus
        - 4.0 * velocity
        + z_padded[2:]
        + z_padded[:-2]
        - 2.0 * velocity
    )
    slope_x = jnp.pad(0.5 * (x_plus - x_minus), ((1, 1), (0, 0), (0, 0)))
    slope_y = jnp.pad(0.5 * (y_plus - y_minus), ((1, 1), (0, 0), (0, 0)))
    mixed_x = 0.5 * (slope_x[2:] - slope_x[:-2])
    mixed_y = 0.5 * (slope_y[2:] - slope_y[:-2])
    total = (
        laplace
        + cross_x.astype(jnp.float32) * mixed_x
        + cross_y.astype(jnp.float32) * mixed_y
        + forcing.astype(jnp.float32)
    )
    rhs = (time_step * total).astype(jnp.bfloat16)
    section_one = jnp.einsum(
        "lab,lbk->lak",
        inv_x,
        lax.all_to_all(rhs, "px", split_axis=0, concat_axis=1, tiled=True),
        preferred_element_type=jnp.float32,
    ).astype(jnp.bfloat16)
    y_lines = lax.all_to_all(section_one, "py", split_axis=1, concat_axis=2, tiled=True)
    section_two = jnp.einsum("lxb,lab->lxa", y_lines, inv_y, preferred_element_type=jnp.float32)
    settled = lax.all_to_all(
        lax.all_to_all(section_two, "py", split_axis=2, concat_axis=1, tiled=True),
        "px",
        split_axis=1,
        concat_axis=0,
        tiled=True,
    )
    return velocity + settled


def send(src, dst, send_sem, recv_sem, target):
    return pltpu.make_async_remote_copy(
        src_ref=src,
        dst_ref=dst,
        send_sem=send_sem,
        recv_sem=recv_sem,
        device_id=target,
        device_id_type=pl.DeviceIdType.MESH,
    )


def kernel(
    npx,
    npy,
    vel_hbm,
    frc_hbm,
    cx_hbm,
    cy_hbm,
    ix_hbm,
    iy_hbm,
    out,
    vel,
    frc,
    cx,
    cy,
    ix,
    iy,
    x_send,
    x_recv,
    cx_ends,
    y_send,
    y_recv,
    cy_ends,
    rhs,
    lines,
    relay,
    cross,
    mid,
    two,
    fin,
    fix_send,
    fix_recv,
    row_recv,
    spread,
    delta,
    extra,
    load_sem,
    relay_come,
    x_sent,
    x_come,
    y_sent,
    y_come,
    rhs_send,
    own_send,
    fix_sent,
    fix_come,
    row_come,
    lines_come,
    cross_come,
    pass_send,
    mid_send,
    last_send,
    out_recv,
    ready,
    gate,
):
    me = lax.axis_index("px")
    my = lax.axis_index("py")
    levels, rows, cols = vel.shape
    part = rows // npy
    order_x, order_y = npx * rows, npy * cols
    x_first = lax.rem(me, 2) == 0
    pieces = [(vel_hbm, vel), (frc_hbm, frc), (cx_hbm, cx), (cy_hbm, cy), (ix_hbm, ix), (iy_hbm, iy)]
    loads = [pltpu.make_async_copy(a, b, load_sem.at[i]) for i, (a, b) in enumerate(pieces)]
    for load in loads:
        load.start()

    def whole(ref, sem):
        return pltpu.make_async_copy(ref, ref, sem)

    barrier = pltpu.get_barrier_semaphore()

    def greet(where):
        pl.semaphore_signal(barrier, inc=1, device_id=where, device_id_type=pl.DeviceIdType.MESH)

    twin = me + 1 - 2 * lax.rem(me, 2)
    for step in range(1, npy):
        other = lax.rem(my + step, npy)
        greet({"py": other})
        greet({"px": twin, "py": other})
    for step in range(1, npx):
        greet({"px": lax.rem(me + step, npx)})
    spread[...] = jnp.zeros_like(spread)
    delta[...] = jnp.zeros_like(delta)
    loads[0].wait()
    lane = lax.broadcasted_iota(jnp.int32, (rows, 128), 1)
    zero = jnp.zeros((rows, 128), jnp.float32)

    for level in range(levels):
        x_send[0, level : level + 1, :] = vel[level, 0:1, :]
        x_send[1, level : level + 1, :] = vel[level, rows - 1 : rows, :]
    first, last = zero, zero
    for level in range(levels):
        first = jnp.where(lane == level, vel[level, :, 0:1], first)
        last = jnp.where(lane == level, vel[level, :, cols - 1 : cols], last)
    y_send[0], y_send[1] = jnp.transpose(first)[:levels], jnp.transpose(last)[:levels]
    pl.semaphore_wait(barrier, npx - 1 + 2 * (npy - 1))

    up_x, down_x = lax.rem(me + 1, npx), lax.rem(me + npx - 1, npx)
    up_y, down_y = lax.rem(my + 1, npy), lax.rem(my + npy - 1, npy)
    halos_y = [
        send(y_send.at[1], y_recv.at[0], y_sent, y_come, {"py": up_y}),
        send(y_send.at[0], y_recv.at[1], y_sent, y_come, {"py": down_y}),
    ]
    halos_x = [
        send(x_send.at[1], x_recv.at[0], x_sent, x_come, {"px": up_x}),
        send(x_send.at[0], x_recv.at[1], x_sent, x_come, {"px": down_x}),
    ]
    for halo in halos_y + halos_x:
        halo.start()
    for step in range(2, npy - 1):
        pl.semaphore_signal(
            ready, inc=1, device_id={"py": lax.rem(my + step, npy)}, device_id_type=pl.DeviceIdType.MESH
        )
    for load in loads[1:4]:
        load.wait()

    def strip(at):
        return pl.ds(pl.multiple_of(at * cols, cols), cols)

    def rows_of(at):
        return pl.ds(pl.multiple_of(at * part, part), part)

    def inner(level):
        now = vel[level]
        above = jnp.where(level < levels - 1, 1.0, 0.0) * vel[jnp.minimum(level + 1, levels - 1)]
        below = jnp.where(level > 0, 1.0, 0.0) * vel[jnp.maximum(level - 1, 0)]
        rise = above - below
        total = pltpu.roll(now, 1, 0) + pltpu.roll(now, rows - 1, 0) + pltpu.roll(now, 1, 1) + pltpu.roll(now, cols - 1, 1)
        total += above + below - 6.0 * now + frc[level].astype(jnp.float32)
        total += cx[level].astype(jnp.float32) * (0.25 * (pltpu.roll(rise, rows - 1, 0) - pltpu.roll(rise, 1, 0)))
        total += cy[level].astype(jnp.float32) * (0.25 * (pltpu.roll(rise, cols - 1, 1) - pltpu.roll(rise, 1, 1)))
        rhs[level] = (time_step * total).astype(jnp.bfloat16)

    def to_cross(level, other):
        src, dst = rhs.at[level, rows_of(other), :], cross.at[me, :, strip(my)]

        def away(sem):
            return send(src, dst, sem, cross_come, {"px": level, "py": other})

        @pl.when(level != me)
        def _():
            away(rhs_send).start()

        @pl.when((level == me) & (other != my))
        def _():
            away(own_send).start()

        @pl.when((level == me) & (other == my))
        def _():
            pltpu.make_async_copy(src, dst, cross_come).start()

    def gap(source, target):
        return lax.rem(source - target + npy, npy) - 1

    def to_relay(at, level, other):
        send(
            rhs.at[level, rows_of(other), :],
            relay.at[at, gap(my, other), lax.rem(me, 2)],
            rhs_send,
            relay_come.at[at],
            {"px": 2 * (me // 2) + 1, "py": other},
        ).start()

    turn = jnp.where(my < npy // 2, 1, npy - 1)

    def mate(step):
        return lax.rem(my + step * turn, npy)

    outermost = (my == 0) | (my == npy - 1)
    ahead = [*range(1, npy)]
    swapped = [*ahead[1::-1], *ahead[2:]]

    def peers(inner):
        return [mate(jnp.where(outermost, *steps)) for steps in zip(ahead, inner)]

    def to_lines(level):
        @pl.when(level != me)
        def _():
            send(rhs.at[level], lines.at[me], rhs_send, lines_come, {"px": level}).start()

        @pl.when(level == me)
        def _():
            pltpu.make_async_copy(rhs.at[level], lines.at[me], lines_come).start()

    pairs = npx // 2

    def level_of(at, odd):
        return 2 * lax.rem(me // 2 + 1 + at, pairs) + odd

    here = level_of(pairs - 1, 1)

    def one_pair(at, _):
        odd = level_of(at, 1)
        inner(odd)
        for other in peers(swapped):
            to_relay(at, odd, other)
        even = level_of(at, 0)
        inner(even)
        to_lines(even)
        return 0

    def near_odd(at, _):
        to_cross(level_of(at, 1), my)
        return 0

    lax.fori_loop(0, pairs - 1, one_pair, 0)
    inner(here - 1)
    to_lines(here - 1)
    inner(here)
    def level_slope(face):
        at = lax.broadcasted_iota(jnp.int32, face.shape, 0)
        lower = jnp.where(at == 0, 0.0, pltpu.roll(face, 1, 0))
        upper = jnp.where(at == levels - 1, 0.0, pltpu.roll(face, levels - 1, 0))
        return 0.25 * (upper - lower)

    pick_row = lax.broadcasted_iota(jnp.int32, (16, cols), 0)
    pick_col = lax.broadcasted_iota(jnp.int32, (16, cols), 1)
    pick = ((pick_row == 0) & (pick_col == 0)) | ((pick_row == 1) & (pick_col == cols - 1))
    picked = lax.dot_general(
        pick.astype(jnp.bfloat16), cy[...].reshape(levels * rows, cols), (((1,), (1,)), ((), ())), preferred_element_type=jnp.float32
    )
    for end in range(2):
        for level in range(levels):
            cy_ends[end, level : level + 1, :] = picked[end : end + 1, level * rows : (level + 1) * rows]
    for level in range(levels):
        cx_ends[0, level : level + 1, :] = cx[level, 0:16, :].astype(jnp.float32)[0:1]
        cx_ends[1, level : level + 1, :] = cx[level, rows - 16 : rows, :].astype(jnp.float32)[15:16]

    def correct(end, came, gone, metric, lanes):
        face = came[end] - gone[1 - end]
        mixed = level_slope(face) if end else -level_slope(face)
        value = time_step * (face + metric[end] * mixed)
        for level in range(levels):
            fix_send[level, end : end + 1, lanes] = value[level : level + 1, :]

    def row_to(level):
        return send(fix_send.at[level, :, pl.ds(rows, cols)], row_recv.at[me], fix_sent, row_come, {"px": level})

    def give_row(at, _):
        level = level_of(at, 0)

        @pl.when(level != me)
        def _():
            row_to(level).start()

        @pl.when(level == me)
        def _():
            pltpu.make_async_copy(fix_send.at[level, :, pl.ds(rows, cols)], row_recv.at[me], row_come).start()

        return 0

    whole(x_recv, x_come).wait()
    for end in range(2):
        correct(end, x_recv, x_send, cx_ends, slice(rows, rows + cols))
    lax.fori_loop(0, pairs, give_row, 0)
    whole(y_recv, y_come).wait()
    for end in range(2):
        correct(end, y_recv, y_send, cy_ends, slice(0, rows))
    if npy > 3:
        pl.semaphore_wait(ready, npy - 3)

    def fix_to(level, other, sem, lanes):
        return send(
            fix_send.at[level, :, pl.ds(0, lanes)],
            fix_recv.at[my, me, :, pl.ds(0, lanes)],
            sem,
            fix_come,
            {"px": level, "py": other},
        )

    def fix_here(level, lanes):
        pltpu.make_async_copy(
            fix_send.at[level, :, pl.ds(0, lanes)], fix_recv.at[my, me, :, pl.ds(0, lanes)], fix_come
        ).start()

    def fix_lanes(other, odd):
        return rows + cols if odd and other in (0, npy - 1) else rows

    def give(at, odd):
        level = level_of(at, odd)
        for other in range(npy):
            mine = (level == me) & (other == my)

            @pl.when(jnp.logical_not(mine))
            def _():
                fix_to(level, other, fix_sent, fix_lanes(other, odd)).start()

            @pl.when(mine)
            def _():
                fix_here(level, fix_lanes(other, odd))

        return 0

    lax.fori_loop(0, pairs, lambda at, _: give(at, 0), 0)
    lax.fori_loop(0, pairs, lambda at, _: give(at, 1), 0)
    for step in range(npy - 1, -1, -1):
        to_cross(here, mate(step))
    lax.fori_loop(0, pairs - 1, near_odd, 0)

    order = [*range(1, npy), 0]
    def narrow(value, shape):
        return value.astype(jnp.bfloat16).reshape(shape)

    def prepare(matrix):
        for q in range(npy):
            for p in range(npx):
                spread[2 * q : 2 * q + 2, p * rows : (p + 1) * rows] = fix_recv[q, p, :, 0:rows]
        moved = lax.dot_general(
            spread[...].astype(jnp.bfloat16), matrix, (((1,), (1,)), ((), ())), preferred_element_type=jnp.float32
        )
        spare = jnp.zeros((128 - moved.shape[0], moved.shape[1]), jnp.float32)
        moved = jnp.transpose(jnp.concatenate([moved, spare], axis=0))
        spot = lax.broadcasted_iota(jnp.int32, moved.shape, 1)
        for q in range(npy):
            for end in range(2):
                tile = slice(q * cols + (cols - 128) * end, q * cols + (cols - 128) * end + 128)
                column = moved[:, 2 * q + end : 2 * q + end + 1]
                now = delta[:, tile].astype(jnp.float32)
                delta[:, tile] = (now + jnp.where(spot == 127 * end, column, 0.0)).astype(jnp.bfloat16)

    def across(ref, other):
        return lax.dot_general(
            ref, iy[strip(other), :], (((1,), (1,)), ((), ())), preferred_element_type=jnp.float32
        )

    def prepare_extra():
        loads[5].wait()

        def one(q, _):
            extra[q] = across(delta[...], q)
            return 0

        lax.fori_loop(0, npy, one, 0)

    def mend_row(ref, at, first, end, where_cols, value):
        spot = lax.broadcasted_iota(jnp.int32, (16, cols), 0) == 15 * end
        block = (*at, slice(first, first + 16), slice(where_cols, where_cols + cols))
        ref[block] = (ref[block].astype(jnp.float32) + jnp.where(spot, value, 0.0)).astype(jnp.bfloat16)

    def mid_to_cross(other, source):
        return send(mid.at[other], cross.at[:, :, strip(source)], mid_send, cross_come, {"py": other})

    def mid_to_lines(other, source):
        return send(mid.at[other], lines.at[:, rows_of(source), :], mid_send, lines_come, {"py": other})

    def pass_on(at, core, source):
        send(
            relay.at[at, gap(source, my), core],
            cross.at[2 * (me // 2) + core, :, strip(source)],
            pass_send,
            cross_come,
            {"px": level_of(at, 1)},
        ).start()

    def two_to(other_y, other_x, sem):
        return send(
            two.at[other_y * npx + other_x], out.at[me, rows_of(my), :], sem, out_recv, {"px": other_x, "py": other_y}
        )

    def fin_to(other):
        return send(fin.at[other], out.at[me], last_send, out_recv, {"px": other})

    def away_px(body):
        def one_step(at, _):
            body(lax.rem(2 * (me // 2) + at, npx))
            return 0

        lax.fori_loop(2, npx, one_step, 0)

    def over_px(body):
        def one_step(at, _):
            body(lax.rem(me + at, npx))
            return 0

        lax.fori_loop(1, npx, one_step, 0)

    @pl.when(x_first)
    def _():
        whole(lines, lines_come).wait()
        whole(row_recv, row_come).wait()
        for p in range(npx):
            for end in range(2):
                mend_row(lines, (p,), (rows - 16) * end, end, 0, row_recv[p, end : end + 1, :])
        loads[4].wait()
        for other in (*peers(swapped), None):
            step, other = other is not None, my if other is None else other
            mine = ix[:, rows_of(other), :].reshape(npx * part, order_x)
            value = jnp.dot(mine, lines[...].reshape(order_x, cols), preferred_element_type=jnp.float32)
            mid[other] = narrow(value, (npx, part, cols))
            if step:
                mid_to_cross(other, my).start()
            else:
                pltpu.make_async_copy(mid.at[my], cross.at[:, :, strip(my)], cross_come).start()
        whole(fix_recv.at[:, :, :, pl.ds(0, rows)], fix_come).wait()
        prepare(ix[:, rows_of(my), :].reshape(npx * part, order_x))
        prepare_extra()
        whole(mid.at[pl.ds(0, npy - 1)], mid_send).wait()
        whole(cross, cross_come).wait()
        for step in (0, *order[:-1]):
            other = mate(step)
            value = across(cross[...].reshape(npx * part, order_y), other) + extra[other]
            two[pl.ds(other * npx, npx)] = narrow(value, (npx, part, cols))
            if not step:
                over_px(lambda other_x: two_to(my, other_x, last_send).start())
                pltpu.make_async_copy(two.at[my * npx + me], out.at[me, rows_of(my), :], out_recv).start()
        first, *rest = peers(ahead[::-1])

        def near_of(other):
            two_to(other, twin, last_send).start()
            two_to(other, me, last_send).start()

        def away_of(other):
            away_px(lambda other_x: two_to(other, other_x, last_send).start())

        @pl.when(jnp.logical_not(outermost))
        def _():
            near_of(first)
            away_of(first)

        pl.semaphore_wait(gate, 1)

        @pl.when(outermost)
        def _():
            near_of(first)

        for other in rest:
            near_of(other)

        @pl.when(outermost)
        def _():
            away_of(first)

        for other in rest:
            away_of(other)

    @pl.when(jnp.logical_not(x_first))
    def _():
        def pass_level(at, _):
            whole(relay.at[at], relay_come.at[at]).wait()
            for step in range(1, npy):
                for core in range(2):
                    pass_on(at, core, mate(step))
            return 0

        lax.fori_loop(0, pairs - 1, pass_level, 0)
        outer = (my == 0) | (my == npy - 1)

        @pl.when(outer)
        def _():
            whole(fix_recv, fix_come).wait()

        @pl.when(jnp.logical_not(outer))
        def _():
            whole(fix_recv.at[:, :, :, pl.ds(0, rows)], fix_come).wait()

        line = lax.broadcasted_iota(jnp.int32, (npx * part, order_x), 0)
        column = lax.broadcasted_iota(jnp.int32, (npx * part, order_x), 1)
        prepare((column == line // part * rows + my * part + lax.rem(line, part)).astype(jnp.bfloat16))
        for end in range(2):
            @pl.when(my == (npy - 1) * end)
            def _():
                for q in range(npy):
                    for p in range(npx):
                        value = fix_recv[q, p, end : end + 1, rows : rows + cols]
                        mend_row(delta, (), p * part + (part - 16) * end, end, q * cols, value)

        prepare_extra()
        whole(cross, cross_come).wait()
        for other in (*peers(swapped), None):
            step, other = other is not None, my if other is None else other
            value = across(cross[...].reshape(npx * part, order_y), other) + extra[other]
            mid[other] = narrow(value, (npx, part, cols))
            if step:
                mid_to_lines(other, my).start()
        pltpu.make_async_copy(mid.at[my], lines.at[:, rows_of(my), :], lines_come).start()
        whole(mid.at[pl.ds(0, npy - 1)], mid_send).wait()
        pl.semaphore_signal(gate, inc=1, device_id={"px": twin}, device_id_type=pl.DeviceIdType.MESH)
        loads[4].wait()
        whole(lines, lines_come).wait()
        half = npx // pairs
        for at in range(pairs):
            first = half * lax.rem(me // half + 1 + at, pairs)
            value = jnp.dot(
                ix[pl.ds(first, half)].reshape(half * rows, order_x),
                lines[...].reshape(order_x, cols),
                preferred_element_type=jnp.float32,
            )
            fin[pl.ds(first, half)] = narrow(value, (half, rows, cols))
            for other in (first, first + 1):
                @pl.when(other != me)
                def _():
                    fin_to(other).start()

                @pl.when(other == me)
                def _():
                    pltpu.make_async_copy(fin.at[me], out.at[me], out_recv).start()

    whole(x_send, x_sent).wait()
    whole(y_send, y_sent).wait()

    whole(rhs.at[pl.ds(0, levels - 1)], rhs_send).wait()

    def fix_done(level, _):
        odd = lax.rem(level, 2)

        @pl.when((level != me) & (odd == 0))
        def _():
            row_to(level).wait_send()

        for kind in range(2):
            for plane in range(npy):
                @pl.when((odd == kind) & ((level != me) | (plane != my)))
                def _():
                    fix_to(level, plane, fix_sent, fix_lanes(plane, kind)).wait_send()

        return 0

    lax.fori_loop(0, levels, fix_done, 0)

    @pl.when(x_first)
    def _():
        whole(two.at[pl.ds(0, npy * npx - 1)], last_send).wait()

    @pl.when(jnp.logical_not(x_first))
    def _():
        whole(rhs.at[me, pl.ds(0, rows - part)], own_send).wait()
        whole(relay, pass_send).wait()
        whole(fin.at[pl.ds(0, npx - 1)], last_send).wait()

    whole(out, out_recv).wait()


def fused(velocity, forcing, cross_x, cross_y, inv_x, inv_y):
    npx, npy = lax.axis_size("px"), lax.axis_size("py")
    levels, rows, cols = velocity.shape
    part = rows // npy
    shape, narrow = velocity.shape, jnp.bfloat16
    order_x, order_y = npx * rows, npy * cols
    vmem, dma = pltpu.VMEM, pltpu.SemaphoreType.DMA
    settled = pl.pallas_call(
        functools.partial(kernel, npx, npy),
        out_shape=jax.ShapeDtypeStruct(shape, narrow),
        in_specs=[pl.BlockSpec(memory_space=pl.ANY)] * 6,
        out_specs=pl.BlockSpec(memory_space=pl.ANY),
        scratch_shapes=[
            vmem(shape, jnp.float32),
            vmem(shape, narrow),
            vmem(shape, narrow),
            vmem(shape, narrow),
            vmem((npx, rows, order_x), narrow),
            vmem((order_y, order_y), narrow),
            vmem((2, levels, cols), jnp.float32),
            vmem((2, levels, cols), jnp.float32),
            vmem((2, levels, cols), jnp.float32),
            vmem((2, levels, rows), jnp.float32),
            vmem((2, levels, rows), jnp.float32),
            vmem((2, levels, rows), jnp.float32),
            vmem((levels, rows, cols), narrow),
            vmem((npx, rows, cols), narrow),
            vmem((npx // 2 - 1, npy - 1, 2, part, cols), narrow),
            vmem((npx, part, order_y), narrow),
            vmem((npy, npx, part, cols), narrow),
            vmem((npy * npx, part, cols), narrow),
            vmem((npx, rows, cols), narrow),
            vmem((levels, 2, rows + cols), jnp.float32),
            vmem((npy, npx, 2, rows + cols), jnp.float32),
            vmem((npx, 2, cols), jnp.float32),
            vmem((-(-2 * npy // 16) * 16, order_x), jnp.float32),
            vmem((npx * part, order_y), narrow),
            vmem((npy, npx * part, cols), jnp.float32),
            dma((6,)),
            dma((npx // 2 - 1,)),
            *[dma] * 15,
            *[pltpu.SemaphoreType.REGULAR] * 2,
        ],
        compiler_params=pltpu.CompilerParams(collective_id=0, has_side_effects=True, vmem_limit_bytes=56_000_000),
        cost_estimate=pl.CostEstimate(flops=4 * order_x * order_y * rows, bytes_accessed=8 * 1024 * 1024, transcendentals=0),
    )(
        velocity,
        forcing,
        cross_x,
        cross_y,
        inv_x.reshape(npx, rows, order_x),
        inv_y.reshape(order_y, order_y),
    )
    return velocity + settled.astype(jnp.float32)


def step(velocity, forcing, cross_x, cross_y, inv_x, inv_y):
    npx, npy = lax.axis_size("px"), lax.axis_size("py")
    levels, rows, cols = velocity.shape
    aligned = rows % (32 * npy) == 0 and rows % 128 == 0 and cols % 128 == 0 and levels % 8 == 0
    paired = npx % 2 == 0 and npx > 2 and npy > 1 and 2 * npy <= 128
    if aligned and paired and levels == npx and inv_x.shape[0] == 1:
        return fused(velocity, forcing, cross_x, cross_y, inv_x, inv_y)
    return shards(velocity, forcing, cross_x, cross_y, inv_x, inv_y)


def solution(mesh):
    return jax.shard_map(
        step,
        mesh=mesh,
        in_specs=(
            P(None, "px", "py"),
            P(None, "px", "py"),
            P(None, "px", "py"),
            P(None, "px", "py"),
            P("px", None, None),
            P("px", None, None),
        ),
        out_specs=P(None, "px", "py"),
        check_vma=False,
    )
```

```python
import functools

import jax
import jax.numpy as jnp
from jax import lax
from jax.experimental import pallas as pl
from jax.experimental.pallas import tpu as pltpu
from jax.sharding import PartitionSpec as P

time_step = 0.25


def with_halo(cells, sides, width):
    for axis, dim in sides:
        count = lax.axis_size(axis)
        head = lax.slice_in_dim(cells, 0, width, axis=dim)
        tail = lax.slice_in_dim(cells, cells.shape[dim] - width, cells.shape[dim], axis=dim)
        cells = jnp.concatenate(
            [
                lax.ppermute(tail, axis, [(i, (i + 1) % count) for i in range(count)]),
                cells,
                lax.ppermute(head, axis, [((i + 1) % count, i) for i in range(count)]),
            ],
            axis=dim,
        )
    return cells


def shards(velocity, forcing, cross_x, cross_y, inv_x, inv_y):
    padded = with_halo(velocity, (("px", 1), ("py", 2)), 1)
    x_plus = padded[:, 2:, 1:-1]
    x_minus = padded[:, :-2, 1:-1]
    y_plus = padded[:, 1:-1, 2:]
    y_minus = padded[:, 1:-1, :-2]
    z_padded = jnp.pad(velocity, ((1, 1), (0, 0), (0, 0)))
    laplace = (
        x_plus
        + x_minus
        + y_plus
        + y_minus
        - 4.0 * velocity
        + z_padded[2:]
        + z_padded[:-2]
        - 2.0 * velocity
    )
    slope_x = jnp.pad(0.5 * (x_plus - x_minus), ((1, 1), (0, 0), (0, 0)))
    slope_y = jnp.pad(0.5 * (y_plus - y_minus), ((1, 1), (0, 0), (0, 0)))
    mixed_x = 0.5 * (slope_x[2:] - slope_x[:-2])
    mixed_y = 0.5 * (slope_y[2:] - slope_y[:-2])
    total = (
        laplace
        + cross_x.astype(jnp.float32) * mixed_x
        + cross_y.astype(jnp.float32) * mixed_y
        + forcing.astype(jnp.float32)
    )
    rhs = (time_step * total).astype(jnp.bfloat16)
    section_one = jnp.einsum(
        "lab,lbk->lak",
        inv_x,
        lax.all_to_all(rhs, "px", split_axis=0, concat_axis=1, tiled=True),
        preferred_element_type=jnp.float32,
    ).astype(jnp.bfloat16)
    y_lines = lax.all_to_all(section_one, "py", split_axis=1, concat_axis=2, tiled=True)
    section_two = jnp.einsum("lxb,lab->lxa", y_lines, inv_y, preferred_element_type=jnp.float32)
    settled = lax.all_to_all(
        lax.all_to_all(section_two, "py", split_axis=2, concat_axis=1, tiled=True),
        "px",
        split_axis=1,
        concat_axis=0,
        tiled=True,
    )
    return velocity + settled


def send(src, dst, send_sem, recv_sem, target):
    return pltpu.make_async_remote_copy(
        src_ref=src,
        dst_ref=dst,
        send_sem=send_sem,
        recv_sem=recv_sem,
        device_id=target,
        device_id_type=pl.DeviceIdType.MESH,
    )


def kernel(
    npx,
    npy,
    vel_hbm,
    frc_hbm,
    cx_hbm,
    cy_hbm,
    ix_hbm,
    iy_hbm,
    out,
    vel,
    frc,
    cx,
    cy,
    ix,
    iy,
    x_send,
    x_recv,
    cx_ends,
    y_send,
    y_recv,
    cy_ends,
    rhs,
    lines,
    relay,
    cross,
    mid,
    two,
    fin,
    fix_send,
    fix_recv,
    row_recv,
    spread,
    delta,
    extra,
    load_sem,
    relay_come,
    x_sent,
    x_come,
    y_sent,
    y_come,
    rhs_send,
    own_send,
    fix_sent,
    fix_come,
    row_come,
    lines_come,
    cross_come,
    pass_send,
    mid_send,
    last_send,
    out_recv,
    ready,
    gate,
):
    me = lax.axis_index("px")
    my = lax.axis_index("py")
    levels, rows, cols = vel.shape
    part = rows // npy
    order_x, order_y = npx * rows, npy * cols
    x_first = lax.rem(me, 2) == 0
    pieces = [(vel_hbm, vel), (frc_hbm, frc), (cx_hbm, cx), (cy_hbm, cy), (ix_hbm, ix), (iy_hbm, iy)]
    loads = [pltpu.make_async_copy(a, b, load_sem.at[i]) for i, (a, b) in enumerate(pieces)]
    for load in loads:
        load.start()

    def whole(ref, sem):
        return pltpu.make_async_copy(ref, ref, sem)

    barrier = pltpu.get_barrier_semaphore()

    def greet(where):
        pl.semaphore_signal(barrier, inc=1, device_id=where, device_id_type=pl.DeviceIdType.MESH)

    twin = me + 1 - 2 * lax.rem(me, 2)
    for step in range(1, npy):
        other = lax.rem(my + step, npy)
        greet({"py": other})
        greet({"px": twin, "py": other})
    for step in range(1, npx):
        greet({"px": lax.rem(me + step, npx)})
    spread[...] = jnp.zeros_like(spread)
    delta[...] = jnp.zeros_like(delta)
    loads[0].wait()
    lane = lax.broadcasted_iota(jnp.int32, (rows, 128), 1)
    zero = jnp.zeros((rows, 128), jnp.float32)

    for level in range(levels):
        x_send[0, level : level + 1, :] = vel[level, 0:1, :]
        x_send[1, level : level + 1, :] = vel[level, rows - 1 : rows, :]
    first, last = zero, zero
    for level in range(levels):
        first = jnp.where(lane == level, vel[level, :, 0:1], first)
        last = jnp.where(lane == level, vel[level, :, cols - 1 : cols], last)
    y_send[0], y_send[1] = jnp.transpose(first)[:levels], jnp.transpose(last)[:levels]
    pl.semaphore_wait(barrier, npx - 1 + 2 * (npy - 1))

    up_x, down_x = lax.rem(me + 1, npx), lax.rem(me + npx - 1, npx)
    up_y, down_y = lax.rem(my + 1, npy), lax.rem(my + npy - 1, npy)
    halos_y = [
        send(y_send.at[1], y_recv.at[0], y_sent, y_come, {"py": up_y}),
        send(y_send.at[0], y_recv.at[1], y_sent, y_come, {"py": down_y}),
    ]
    halos_x = [
        send(x_send.at[1], x_recv.at[0], x_sent, x_come, {"px": up_x}),
        send(x_send.at[0], x_recv.at[1], x_sent, x_come, {"px": down_x}),
    ]
    for halo in halos_y + halos_x:
        halo.start()
    for step in range(2, npy - 1):
        pl.semaphore_signal(
            ready, inc=1, device_id={"py": lax.rem(my + step, npy)}, device_id_type=pl.DeviceIdType.MESH
        )
    for load in loads[1:4]:
        load.wait()

    def strip(at):
        return pl.ds(pl.multiple_of(at * cols, cols), cols)

    def rows_of(at):
        return pl.ds(pl.multiple_of(at * part, part), part)

    def inner(level):
        now = vel[level]
        above = jnp.where(level < levels - 1, 1.0, 0.0) * vel[jnp.minimum(level + 1, levels - 1)]
        below = jnp.where(level > 0, 1.0, 0.0) * vel[jnp.maximum(level - 1, 0)]
        rise = above - below
        total = pltpu.roll(now, 1, 0) + pltpu.roll(now, rows - 1, 0) + pltpu.roll(now, 1, 1) + pltpu.roll(now, cols - 1, 1)
        total += above + below - 6.0 * now + frc[level].astype(jnp.float32)
        total += cx[level].astype(jnp.float32) * (0.25 * (pltpu.roll(rise, rows - 1, 0) - pltpu.roll(rise, 1, 0)))
        total += cy[level].astype(jnp.float32) * (0.25 * (pltpu.roll(rise, cols - 1, 1) - pltpu.roll(rise, 1, 1)))
        rhs[level] = (time_step * total).astype(jnp.bfloat16)

    def to_cross(level, other):
        src, dst = rhs.at[level, rows_of(other), :], cross.at[me, :, strip(my)]

        def away(sem):
            return send(src, dst, sem, cross_come, {"px": level, "py": other})

        @pl.when(level != me)
        def _():
            away(rhs_send).start()

        @pl.when((level == me) & (other != my))
        def _():
            away(own_send).start()

        @pl.when((level == me) & (other == my))
        def _():
            pltpu.make_async_copy(src, dst, cross_come).start()

    def gap(source, target):
        return lax.rem(source - target + npy, npy) - 1

    def to_relay(at, level, other):
        send(
            rhs.at[level, rows_of(other), :],
            relay.at[at, gap(my, other), lax.rem(me, 2)],
            rhs_send,
            relay_come.at[at, gap(my, other)],
            {"px": 2 * (me // 2) + 1, "py": other},
        ).start()

    turn = jnp.where(my < npy // 2, 1, npy - 1)

    def mate(step):
        return lax.rem(my + step * turn, npy)

    outermost = (my == 0) | (my == npy - 1)
    ahead = [*range(1, npy)]
    swapped = [*ahead[1::-1], *ahead[2:]]

    def peers(inner):
        return [mate(jnp.where(outermost, *steps)) for steps in zip(ahead, inner)]

    def to_lines(level):
        @pl.when(level != me)
        def _():
            send(rhs.at[level], lines.at[me], rhs_send, lines_come, {"px": level}).start()

        @pl.when(level == me)
        def _():
            pltpu.make_async_copy(rhs.at[level], lines.at[me], lines_come).start()

    pairs = npx // 2

    def level_of(at, odd):
        return 2 * lax.rem(me // 2 + 1 + at, pairs) + odd

    here = level_of(pairs - 1, 1)

    def one_pair(at, _):
        odd = level_of(at, 1)
        inner(odd)
        for other in peers(swapped):
            to_relay(at, odd, other)
        even = level_of(at, 0)
        inner(even)
        to_lines(even)
        return 0

    def near_odd(at, _):
        to_cross(level_of(at, 1), my)
        return 0

    lax.fori_loop(0, pairs - 1, one_pair, 0)
    inner(here - 1)
    to_lines(here - 1)
    inner(here)
    def level_slope(face):
        at = lax.broadcasted_iota(jnp.int32, face.shape, 0)
        lower = jnp.where(at == 0, 0.0, pltpu.roll(face, 1, 0))
        upper = jnp.where(at == levels - 1, 0.0, pltpu.roll(face, levels - 1, 0))
        return 0.25 * (upper - lower)

    pick_row = lax.broadcasted_iota(jnp.int32, (16, cols), 0)
    pick_col = lax.broadcasted_iota(jnp.int32, (16, cols), 1)
    pick = ((pick_row == 0) & (pick_col == 0)) | ((pick_row == 1) & (pick_col == cols - 1))
    picked = lax.dot_general(
        pick.astype(jnp.bfloat16), cy[...].reshape(levels * rows, cols), (((1,), (1,)), ((), ())), preferred_element_type=jnp.float32
    )
    for end in range(2):
        for level in range(levels):
            cy_ends[end, level : level + 1, :] = picked[end : end + 1, level * rows : (level + 1) * rows]
    for level in range(levels):
        cx_ends[0, level : level + 1, :] = cx[level, 0:16, :].astype(jnp.float32)[0:1]
        cx_ends[1, level : level + 1, :] = cx[level, rows - 16 : rows, :].astype(jnp.float32)[15:16]

    def correct(end, came, gone, metric, lanes):
        face = came[end] - gone[1 - end]
        mixed = level_slope(face) if end else -level_slope(face)
        value = time_step * (face + metric[end] * mixed)
        for level in range(levels):
            fix_send[level, end : end + 1, lanes] = value[level : level + 1, :]

    def row_to(level):
        return send(fix_send.at[level, :, pl.ds(rows, cols)], row_recv.at[me], fix_sent, row_come, {"px": level})

    def give_row(at, _):
        level = level_of(at, 0)

        @pl.when(level != me)
        def _():
            row_to(level).start()

        @pl.when(level == me)
        def _():
            pltpu.make_async_copy(fix_send.at[level, :, pl.ds(rows, cols)], row_recv.at[me], row_come).start()

        return 0

    whole(x_recv, x_come).wait()
    for end in range(2):
        correct(end, x_recv, x_send, cx_ends, slice(rows, rows + cols))
    lax.fori_loop(0, pairs, give_row, 0)
    whole(y_recv, y_come).wait()
    for end in range(2):
        correct(end, y_recv, y_send, cy_ends, slice(0, rows))
    if npy > 3:
        pl.semaphore_wait(ready, npy - 3)

    def fix_to(level, other, sem, lanes):
        return send(
            fix_send.at[level, :, pl.ds(0, lanes)],
            fix_recv.at[my, me, :, pl.ds(0, lanes)],
            sem,
            fix_come,
            {"px": level, "py": other},
        )

    def fix_here(level, lanes):
        pltpu.make_async_copy(
            fix_send.at[level, :, pl.ds(0, lanes)], fix_recv.at[my, me, :, pl.ds(0, lanes)], fix_come
        ).start()

    def fix_lanes(other, odd):
        return rows + cols if odd and other in (0, npy - 1) else rows

    def give(at, odd):
        level = level_of(at, odd)
        for other in range(npy):
            mine = (level == me) & (other == my)

            @pl.when(jnp.logical_not(mine))
            def _():
                fix_to(level, other, fix_sent, fix_lanes(other, odd)).start()

            @pl.when(mine)
            def _():
                fix_here(level, fix_lanes(other, odd))

        return 0

    lax.fori_loop(0, pairs, lambda at, _: give(at, 0), 0)
    lax.fori_loop(0, pairs, lambda at, _: give(at, 1), 0)
    for step in range(npy - 1, -1, -1):
        to_cross(here, mate(step))
    lax.fori_loop(0, pairs - 1, near_odd, 0)

    order = [*range(1, npy), 0]
    def narrow(value, shape):
        return value.astype(jnp.bfloat16).reshape(shape)

    def prepare(matrix):
        for q in range(npy):
            for p in range(npx):
                spread[2 * q : 2 * q + 2, p * rows : (p + 1) * rows] = fix_recv[q, p, :, 0:rows]
        moved = lax.dot_general(
            spread[...].astype(jnp.bfloat16), matrix, (((1,), (1,)), ((), ())), preferred_element_type=jnp.float32
        )
        spare = jnp.zeros((128 - moved.shape[0], moved.shape[1]), jnp.float32)
        moved = jnp.transpose(jnp.concatenate([moved, spare], axis=0))
        spot = lax.broadcasted_iota(jnp.int32, moved.shape, 1)
        for q in range(npy):
            for end in range(2):
                tile = slice(q * cols + (cols - 128) * end, q * cols + (cols - 128) * end + 128)
                column = moved[:, 2 * q + end : 2 * q + end + 1]
                now = delta[:, tile].astype(jnp.float32)
                delta[:, tile] = (now + jnp.where(spot == 127 * end, column, 0.0)).astype(jnp.bfloat16)

    def across(ref, other):
        return lax.dot_general(
            ref, iy[strip(other), :], (((1,), (1,)), ((), ())), preferred_element_type=jnp.float32
        )

    def prepare_extra():
        loads[5].wait()

        def one(q, _):
            extra[q] = across(delta[...], q)
            return 0

        lax.fori_loop(0, npy, one, 0)

    def mend_row(ref, at, first, end, where_cols, value):
        spot = lax.broadcasted_iota(jnp.int32, (16, cols), 0) == 15 * end
        block = (*at, slice(first, first + 16), slice(where_cols, where_cols + cols))
        ref[block] = (ref[block].astype(jnp.float32) + jnp.where(spot, value, 0.0)).astype(jnp.bfloat16)

    def mid_to_cross(other, source):
        return send(mid.at[other], cross.at[:, :, strip(source)], mid_send, cross_come, {"py": other})

    def mid_to_lines(other, source):
        return send(mid.at[other], lines.at[:, rows_of(source), :], mid_send, lines_come, {"py": other})

    def pass_on(at, core, source):
        send(
            relay.at[at, gap(source, my), core],
            cross.at[2 * (me // 2) + core, :, strip(source)],
            pass_send,
            cross_come,
            {"px": level_of(at, 1)},
        ).start()

    def two_to(other_y, other_x, sem):
        return send(
            two.at[other_y * npx + other_x], out.at[me, rows_of(my), :], sem, out_recv, {"px": other_x, "py": other_y}
        )

    def fin_to(other):
        return send(fin.at[other], out.at[me], last_send, out_recv, {"px": other})

    def away_px(body):
        def one_step(at, _):
            body(lax.rem(2 * (me // 2) + at, npx))
            return 0

        lax.fori_loop(2, npx, one_step, 0)

    def over_px(body):
        def one_step(at, _):
            body(lax.rem(me + at, npx))
            return 0

        lax.fori_loop(1, npx, one_step, 0)

    @pl.when(x_first)
    def _():
        whole(lines, lines_come).wait()
        whole(row_recv, row_come).wait()
        for p in range(npx):
            for end in range(2):
                mend_row(lines, (p,), (rows - 16) * end, end, 0, row_recv[p, end : end + 1, :])
        loads[4].wait()
        for other in (*peers(swapped), None):
            step, other = other is not None, my if other is None else other
            mine = ix[:, rows_of(other), :].reshape(npx * part, order_x)
            value = jnp.dot(mine, lines[...].reshape(order_x, cols), preferred_element_type=jnp.float32)
            mid[other] = narrow(value, (npx, part, cols))
            if step:
                mid_to_cross(other, my).start()
            else:
                pltpu.make_async_copy(mid.at[my], cross.at[:, :, strip(my)], cross_come).start()
        whole(fix_recv.at[:, :, :, pl.ds(0, rows)], fix_come).wait()
        prepare(ix[:, rows_of(my), :].reshape(npx * part, order_x))
        prepare_extra()
        whole(mid.at[pl.ds(0, npy - 1)], mid_send).wait()
        whole(cross, cross_come).wait()
        for step in (0, *order[:-1]):
            other = mate(step)
            value = across(cross[...].reshape(npx * part, order_y), other) + extra[other]
            two[pl.ds(other * npx, npx)] = narrow(value, (npx, part, cols))
            if not step:
                over_px(lambda other_x: two_to(my, other_x, last_send).start())
                pltpu.make_async_copy(two.at[my * npx + me], out.at[me, rows_of(my), :], out_recv).start()
        first, *rest = peers(ahead[::-1])

        def near_of(other):
            two_to(other, twin, last_send).start()
            two_to(other, me, last_send).start()

        def away_of(other):
            away_px(lambda other_x: two_to(other, other_x, last_send).start())

        @pl.when(jnp.logical_not(outermost))
        def _():
            near_of(first)
            away_of(first)

        pl.semaphore_wait(gate, 1)

        @pl.when(outermost)
        def _():
            near_of(first)

        for other in rest:
            near_of(other)

        @pl.when(outermost)
        def _():
            away_of(first)

        for other in rest:
            away_of(other)

    @pl.when(jnp.logical_not(x_first))
    def _():
        def pass_level(at, _):
            for step in range(1, npy):
                spot = (at, gap(mate(step), my))
                whole(relay.at[spot], relay_come.at[spot]).wait()
                for core in range(2):
                    pass_on(at, core, mate(step))
            return 0

        lax.fori_loop(0, pairs - 1, pass_level, 0)
        outer = (my == 0) | (my == npy - 1)

        @pl.when(outer)
        def _():
            whole(fix_recv, fix_come).wait()

        @pl.when(jnp.logical_not(outer))
        def _():
            whole(fix_recv.at[:, :, :, pl.ds(0, rows)], fix_come).wait()

        line = lax.broadcasted_iota(jnp.int32, (npx * part, order_x), 0)
        column = lax.broadcasted_iota(jnp.int32, (npx * part, order_x), 1)
        prepare((column == line // part * rows + my * part + lax.rem(line, part)).astype(jnp.bfloat16))
        for end in range(2):
            @pl.when(my == (npy - 1) * end)
            def _():
                for q in range(npy):
                    for p in range(npx):
                        value = fix_recv[q, p, end : end + 1, rows : rows + cols]
                        mend_row(delta, (), p * part + (part - 16) * end, end, q * cols, value)

        prepare_extra()
        whole(cross, cross_come).wait()
        for other in (*peers(swapped), None):
            step, other = other is not None, my if other is None else other
            value = across(cross[...].reshape(npx * part, order_y), other) + extra[other]
            mid[other] = narrow(value, (npx, part, cols))
            if step:
                mid_to_lines(other, my).start()
        pltpu.make_async_copy(mid.at[my], lines.at[:, rows_of(my), :], lines_come).start()
        whole(mid.at[pl.ds(0, npy - 1)], mid_send).wait()
        pl.semaphore_signal(gate, inc=1, device_id={"px": twin}, device_id_type=pl.DeviceIdType.MESH)
        loads[4].wait()
        whole(lines, lines_come).wait()
        half = npx // pairs
        for at in range(pairs):
            first = half * lax.rem(me // half + 1 + at, pairs)
            value = jnp.dot(
                ix[pl.ds(first, half)].reshape(half * rows, order_x),
                lines[...].reshape(order_x, cols),
                preferred_element_type=jnp.float32,
            )
            fin[pl.ds(first, half)] = narrow(value, (half, rows, cols))
            for other in (first, first + 1):
                @pl.when(other != me)
                def _():
                    fin_to(other).start()

                @pl.when(other == me)
                def _():
                    pltpu.make_async_copy(fin.at[me], out.at[me], out_recv).start()

    whole(x_send, x_sent).wait()
    whole(y_send, y_sent).wait()

    whole(rhs.at[pl.ds(0, levels - 1)], rhs_send).wait()

    def fix_done(level, _):
        odd = lax.rem(level, 2)

        @pl.when((level != me) & (odd == 0))
        def _():
            row_to(level).wait_send()

        for kind in range(2):
            for plane in range(npy):
                @pl.when((odd == kind) & ((level != me) | (plane != my)))
                def _():
                    fix_to(level, plane, fix_sent, fix_lanes(plane, kind)).wait_send()

        return 0

    lax.fori_loop(0, levels, fix_done, 0)

    @pl.when(x_first)
    def _():
        whole(two.at[pl.ds(0, npy * npx - 1)], last_send).wait()

    @pl.when(jnp.logical_not(x_first))
    def _():
        whole(rhs.at[me, pl.ds(0, rows - part)], own_send).wait()
        whole(relay, pass_send).wait()
        whole(fin.at[pl.ds(0, npx - 1)], last_send).wait()

    whole(out, out_recv).wait()


def fused(velocity, forcing, cross_x, cross_y, inv_x, inv_y):
    npx, npy = lax.axis_size("px"), lax.axis_size("py")
    levels, rows, cols = velocity.shape
    part = rows // npy
    shape, narrow = velocity.shape, jnp.bfloat16
    order_x, order_y = npx * rows, npy * cols
    vmem, dma = pltpu.VMEM, pltpu.SemaphoreType.DMA
    settled = pl.pallas_call(
        functools.partial(kernel, npx, npy),
        out_shape=jax.ShapeDtypeStruct(shape, narrow),
        in_specs=[pl.BlockSpec(memory_space=pl.ANY)] * 6,
        out_specs=pl.BlockSpec(memory_space=pl.ANY),
        scratch_shapes=[
            vmem(shape, jnp.float32),
            vmem(shape, narrow),
            vmem(shape, narrow),
            vmem(shape, narrow),
            vmem((npx, rows, order_x), narrow),
            vmem((order_y, order_y), narrow),
            vmem((2, levels, cols), jnp.float32),
            vmem((2, levels, cols), jnp.float32),
            vmem((2, levels, cols), jnp.float32),
            vmem((2, levels, rows), jnp.float32),
            vmem((2, levels, rows), jnp.float32),
            vmem((2, levels, rows), jnp.float32),
            vmem((levels, rows, cols), narrow),
            vmem((npx, rows, cols), narrow),
            vmem((npx // 2 - 1, npy - 1, 2, part, cols), narrow),
            vmem((npx, part, order_y), narrow),
            vmem((npy, npx, part, cols), narrow),
            vmem((npy * npx, part, cols), narrow),
            vmem((npx, rows, cols), narrow),
            vmem((levels, 2, rows + cols), jnp.float32),
            vmem((npy, npx, 2, rows + cols), jnp.float32),
            vmem((npx, 2, cols), jnp.float32),
            vmem((-(-2 * npy // 16) * 16, order_x), jnp.float32),
            vmem((npx * part, order_y), narrow),
            vmem((npy, npx * part, cols), jnp.float32),
            dma((6,)),
            dma((npx // 2 - 1, npy - 1)),
            *[dma] * 15,
            *[pltpu.SemaphoreType.REGULAR] * 2,
        ],
        compiler_params=pltpu.CompilerParams(collective_id=0, has_side_effects=True, vmem_limit_bytes=56_000_000),
        cost_estimate=pl.CostEstimate(flops=4 * order_x * order_y * rows, bytes_accessed=8 * 1024 * 1024, transcendentals=0),
    )(
        velocity,
        forcing,
        cross_x,
        cross_y,
        inv_x.reshape(npx, rows, order_x),
        inv_y.reshape(order_y, order_y),
    )
    return velocity + settled.astype(jnp.float32)


def step(velocity, forcing, cross_x, cross_y, inv_x, inv_y):
    npx, npy = lax.axis_size("px"), lax.axis_size("py")
    levels, rows, cols = velocity.shape
    aligned = rows % (32 * npy) == 0 and rows % 128 == 0 and cols % 128 == 0 and levels % 8 == 0
    paired = npx % 2 == 0 and npx > 2 and npy > 1 and 2 * npy <= 128
    if aligned and paired and levels == npx and inv_x.shape[0] == 1:
        return fused(velocity, forcing, cross_x, cross_y, inv_x, inv_y)
    return shards(velocity, forcing, cross_x, cross_y, inv_x, inv_y)


def solution(mesh):
    return jax.shard_map(
        step,
        mesh=mesh,
        in_specs=(
            P(None, "px", "py"),
            P(None, "px", "py"),
            P(None, "px", "py"),
            P(None, "px", "py"),
            P("px", None, None),
            P("px", None, None),
        ),
        out_specs=P(None, "px", "py"),
        check_vma=False,
    )
```
